256 devices in a mesh: cam: 4 (over y), tile: 64 (over x, z, core).
Axes of the slice: x: 4, y: 4, z: 8, core: 2. Of those that a mesh axis runs over, the one named last changes fastest.
Arguments:
- positions: float32 [3, 262144], P(None, ('cam', 'tile')), may hold values from -1 to 1
- log_scales: float32 [3, 262144], P(None, ('cam', 'tile')), may hold values from -4.5 to -2.5
- rotations: float32 [4, 262144], P(None, ('cam', 'tile')), may hold values from 0.3 to 1
- opacities: float32 [262144], P(('cam', 'tile')), may hold values from -6 to -3
- colors: float32 [48, 262144], P(None, ('cam', 'tile')), may hold values from -3 to 3
- cameras: float32 [2, 4, 6], replicated, may hold values from -0.05 to 0.05
- targets: float32 [2, 4, 64, 3, 256], P(None, 'cam', 'tile'), may hold values from 0 to 1
- tile_ids: int32 [2, 4, 64], P(None, 'cam', 'tile'), may hold values from 8320 to 24448, as said below
- tile_counts: int32 [2, 4, 64], P(None, 'cam', 'tile'), may hold values from 128 to 256, as said below
- tile_lists: int32 [2, 4, 64, 256], P(None, 'cam', 'tile'), may hold values from 0 to 2047, as said below
- fetch_ids: int32 [2, 4, 64, 4, 64, 8], P(None, 'cam', 'tile'), may hold values from 0 to 1023, as said below
Outputs:
- grad_positions: float32 [3, 262144], P(None, ('cam', 'tile'))
- grad_log_scales: float32 [3, 262144], P(None, ('cam', 'tile'))
- grad_rotations: float32 [4, 262144], P(None, ('cam', 'tile'))
- grad_opacities: float32 [262144], P(('cam', 'tile'))
- grad_colors: float32 [48, 262144], P(None, ('cam', 'tile'))
The draws below stay inside these ranges and needn't reach their ends.
Inputs may be any that keep to these rules, and one draw needn't show every extreme that they name: Within one row fetch_ids[p, c, t, a, b, :] the entries are distinct local columns of the owner at cam a, tile b, all within the block of 1024 // 64 columns that belongs to the device's row of tiles; not every slot is named by a list. `tile_lists`: entries are slots of the rendering device, distinct within a tile, in increasing order of the third coordinate of their Gaussians' positions. `tile_counts`: each device has a tile with 256 live entries in each pass. `tile_ids`: each device renders one image tile in a pass; in each pass and camera group the devices' rows are distinct and together form a window of 64 rows.
All inputs are finite; a program needn't handle non-finite values.
Results may differ from the reference program's by a relative error of at most 0.0003.
Values sent between devices are 32-bit elements; how exact they have to be, the bound alone decides.
A program may use at most 192 MiB of HBM per device.

```python
import jax
import jax.numpy as jnp
from jax import lax

G_DEV = 1024
TILES_DEV = 1
PASSES = 2
LIST = 256
PIX = 256
COEFS = 48
CAP = 8
TILES = 64
NG = 262144
N_CAM = 4
N_TILE = 64


def region_ranks(key):
    count = N_CAM * N_TILE * (G_DEV // N_TILE)
    region_keys = jax.random.split(jax.random.fold_in(key, 13), N_TILE)

    def shuffle(region_key):
        return jax.random.permutation(region_key, count)
    return jax.vmap(shuffle)(region_keys).astype(jnp.int32)


def region_layout(key):
    ranks = region_ranks(key)
    seeds = jax.random.split(jax.random.fold_in(key, 11), 6)
    owners = N_CAM * N_TILE
    slots = owners * CAP
    lead = (PASSES, N_CAM, N_TILE)
    per_region = G_DEV // N_TILE
    count = owners * per_region

    def shuffle_rows(row_key):
        return jax.random.permutation(row_key, N_TILE)
    assigned = jax.vmap(shuffle_rows)(jax.random.split(seeds[0], PASSES * N_CAM)).reshape(lead).astype(jnp.int32)
    owner_index = jnp.arange(owners, dtype=jnp.int32)
    usage = jax.random.randint(seeds[1], lead + (owners,), max(1, CAP // 4), CAP + 1, dtype=jnp.int32)
    heavy = jax.random.randint(seeds[2], (PASSES, 1, 1, 1), 0, owners, dtype=jnp.int32)
    usage = jnp.where(owner_index == heavy, CAP, usage)
    extra = jax.random.randint(seeds[3], lead + (1,), 0, owners, dtype=jnp.int32)
    usage = jnp.where(owner_index == extra, CAP, usage)
    usage = usage.at[0, 0, 0, owners - 1].set(CAP)
    limit = 2 ** 31 // (per_region + 1)
    noise = jax.random.randint(seeds[4], lead + (owners, per_region), 0, limit, dtype=jnp.int32)
    scores = noise * per_region + jnp.arange(per_region, dtype=jnp.int32)
    scores = scores.at[0, 0, :, 0, 0].set(2147483647).at[0, 0, :, owners - 1, per_region - 1].set(2147483646)
    unused, within = lax.top_k(scores, CAP)
    within = within.astype(jnp.int32)
    fetched = assigned[..., None, None] * per_region + within
    fetched = fetched.reshape(PASSES, N_CAM, N_TILE, N_CAM, N_TILE, CAP).astype(jnp.int32)
    slot_index = jnp.arange(CAP, dtype=jnp.int32)
    valid = (slot_index < usage[..., None]).reshape(lead + (slots,))
    home = (within % TILES_DEV).reshape(lead + (slots,))
    slot_rank = ranks[assigned[..., None, None], owner_index[:, None] * per_region + within].reshape(lead + (slots,))
    tile_index = jnp.arange(TILES_DEV, dtype=jnp.int32)
    distance = jnp.abs(home[..., None, :] - tile_index[:, None])
    spread = 2 ** 31 // ((TILES_DEV + 1) * (slots + 1))
    jitter = jax.random.randint(seeds[5], lead + (TILES_DEV, slots), 0, spread, dtype=jnp.int32)
    flat_index = jnp.arange(slots, dtype=jnp.int32)
    closeness = ((TILES_DEV - distance) * spread + jitter) * slots + flat_index
    closeness = jnp.where(valid[..., None, :], closeness, -1 - flat_index)
    closeness = closeness.at[0, 0, 0, 0, 0].set(2147483647).at[0, 0, 0, 0, slots - 1].set(2147483646)
    unused, near = lax.top_k(closeness, LIST)
    near = near.astype(jnp.int32)
    near_rank = jnp.take_along_axis(jnp.broadcast_to(slot_rank[..., None, :], lead + (TILES_DEV, slots)), near, axis=-1)
    unused, front = lax.top_k(count - near_rank, LIST)
    chosen = jnp.take_along_axis(near, front.astype(jnp.int32), axis=-1)
    chosen = chosen.reshape(PASSES, N_CAM, N_TILE * TILES_DEV, LIST).astype(jnp.int32)
    first_row = 64 - N_TILE // 2
    first_col = 128 - TILES_DEV // 2
    numbers = (first_row + assigned)[..., None] * 256 + first_col + tile_index
    numbers = numbers.reshape(PASSES, N_CAM, N_TILE * TILES_DEV).astype(jnp.int32)
    return (fetched, chosen, numbers)


def draw_fetch_ids(key, part):
    return region_layout(key)[0]


def draw_tile_lists(key, part):
    return region_layout(key)[1]


def draw_tile_ids(key, part):
    return region_layout(key)[2]


def draw_tile_counts(key, part):
    seeds = jax.random.split(jax.random.fold_in(key, 5), 2)
    counts = jax.random.randint(seeds[0], (PASSES, N_CAM, N_TILE, TILES_DEV), LIST // 2, LIST + 1, dtype=jnp.int32)
    full = jax.random.randint(seeds[1], (PASSES, N_CAM, N_TILE, 1), 0, TILES_DEV, dtype=jnp.int32)
    counts = jnp.where(jnp.arange(TILES_DEV, dtype=jnp.int32) == full, LIST, counts)
    return counts.reshape(PASSES, N_CAM, N_TILE * TILES_DEV).astype(jnp.int32)


def draw_positions(key, part):
    ranks = region_ranks(key)
    owners = N_CAM * N_TILE
    per_region = G_DEV // N_TILE
    count = owners * per_region
    owner_index = jnp.arange(owners, dtype=jnp.int32)[:, None]
    column = jnp.arange(G_DEV, dtype=jnp.int32)[None, :]
    region = column // per_region
    within = column % per_region
    rank = ranks[region, owner_index * per_region + within]
    home_col = jnp.broadcast_to(128 - TILES_DEV // 2 + within % TILES_DEV, (owners, G_DEV)).astype(jnp.float32)
    home_row = jnp.broadcast_to(64 - N_TILE // 2 + region, (owners, G_DEV)).astype(jnp.float32)
    float_keys = jax.random.split(jax.random.fold_in(key, 23), 3)
    shape = (owners, G_DEV)
    shift_x = jax.random.uniform(float_keys[0], shape, jnp.float32, -8.0, 24.0)
    shift_y = jax.random.uniform(float_keys[1], shape, jnp.float32, -8.0, 24.0)
    depth_shift = jax.random.uniform(float_keys[2], shape, jnp.float32, 0.2, 0.8)
    screen_x = 16.0 * home_col + shift_x
    screen_y = 16.0 * home_row + shift_y
    depth = 5.0 + 2.0 * (rank.astype(jnp.float32) + depth_shift) / count
    placed = jnp.stack([(screen_x - 2048.0) * depth / 4096.0, (screen_y - 1024.0) * depth / 4096.0, depth - 6.0])
    return placed.reshape(3, owners * G_DEV).astype(jnp.float32)


def draw_cameras(key, part):
    reach = jnp.array([0.0001, 0.0001, 0.002, 0.01, 0.01, 0.05], dtype=jnp.float32)
    float_keys = jax.random.split(jax.random.fold_in(key, 31), 1)
    shape = (PASSES, N_CAM, 6)
    values = jax.random.uniform(float_keys[0], shape, jnp.float32, -1.0, 1.0)
    return (values * reach).astype(jnp.float32)


def steps_of(own_key, shape, shards, low, largest):
    level, own = 1.0, jax.random.fold_in(own_key, 6)
    for axis_at, parts in shards:
        steps = jnp.exp(jax.random.uniform(jax.random.fold_in(own, axis_at), (parts,), jnp.float32, low / len(shards), largest / len(shards)))
        level = level * jnp.repeat(steps, shape[axis_at] // parts).reshape([-1 if axis == axis_at else 1 for axis in range(len(shape))])
    return level


def centred(rng, shape, scale, most, cuts=(), held_as=jnp.bfloat16):
    values = jax.random.normal(rng, shape, jnp.float32) * scale
    if len(cuts) > 0:
        values = steps_of(rng, shape, cuts, -0.22, 0.18) * values
    return jnp.clip(values, min=-most, max=most).astype(held_as)


def setup_inputs(seed: int = 0) -> dict:
    arg_keys = jax.random.split(jax.random.key(seed), 12)
    positions = draw_positions(jax.random.fold_in(arg_keys[11], 71), 0)
    log_scales = jnp.clip(-4.5 + 2.0 * jax.random.uniform(arg_keys[1], (3, NG), jnp.float32) ** steps_of(arg_keys[1], (3, NG), ((1, 256),), -0.2, 0.2), -4.5, -2.5)
    rotations = jnp.clip(0.3 + 0.7 * jax.random.uniform(arg_keys[2], (4, NG), jnp.float32) ** steps_of(arg_keys[2], (4, NG), ((1, 256),), -0.2, 0.2), 0.3, 1.0)
    opacities = jnp.clip(-6.0 + 3.0 * jax.random.uniform(arg_keys[3], (NG,), jnp.float32) ** steps_of(arg_keys[3], (NG,), ((0, 256),), -0.2, 0.2), -6.0, -3.0)
    colors = centred(arg_keys[4], (COEFS, NG), 0.5, 3.0, ((1, 256),), jnp.float32)
    cameras = draw_cameras(jax.random.fold_in(arg_keys[11], 71), 0)
    targets = jnp.clip(1.0 * jax.random.uniform(arg_keys[6], (PASSES, N_CAM, TILES, 3, PIX), jnp.float32) ** steps_of(arg_keys[6], (PASSES, N_CAM, TILES, 3, PIX), ((1, 4), (2, 64)), -0.2, 0.2), 0.0, 1.0)
    tile_ids = draw_tile_ids(jax.random.fold_in(arg_keys[11], 71), 0)
    tile_counts = draw_tile_counts(jax.random.fold_in(arg_keys[11], 71), 0)
    tile_lists = draw_tile_lists(jax.random.fold_in(arg_keys[11], 71), 0)
    fetch_ids = draw_fetch_ids(jax.random.fold_in(arg_keys[11], 71), 0)
    return {"positions": positions, "log_scales": log_scales, "rotations": rotations, "opacities": opacities, "colors": colors, "cameras": cameras, "targets": targets, "tile_ids": tile_ids, "tile_counts": tile_counts, "tile_lists": tile_lists, "fetch_ids": fetch_ids}


FOCAL = 4096.0
SH_ZERO = 0.28209479177387814
SH_ONE = 0.4886025119029199
SH_TWO = [1.0925484305920792, -1.0925484305920792, 0.31539156525252005, -1.0925484305920792, 0.5462742152960396]
SH_THREE = [-0.5900435899266435, 2.890611442640554, -0.4570457994644658, 0.3731763325901154, -0.4570457994644658, 1.445305721320277, -0.5900435899266435]

def matmul3(left, right):
    return [[left[i][0] * right[0][j] + left[i][1] * right[1][j] + left[i][2] * right[2][j] for j in range(3)] for i in range(3)]

def project(raw, camera):
    cos_a, sin_a = (jnp.cos(camera[0]), jnp.sin(camera[0]))
    cos_b, sin_b = (jnp.cos(camera[1]), jnp.sin(camera[1]))
    cos_c, sin_c = (jnp.cos(camera[2]), jnp.sin(camera[2]))
    turn_x = [[1.0, 0.0, 0.0], [0.0, cos_a, -sin_a], [0.0, sin_a, cos_a]]
    turn_y = [[cos_b, 0.0, sin_b], [0.0, 1.0, 0.0], [-sin_b, 0.0, cos_b]]
    turn_z = [[cos_c, -sin_c, 0.0], [sin_c, cos_c, 0.0], [0.0, 0.0, 1.0]]
    rotate = matmul3(matmul3(turn_z, turn_y), turn_x)
    offset = [camera[3], camera[4], 6.0 + camera[5]]
    point = [raw[0], raw[1], raw[2]]
    viewed = [rotate[i][0] * point[0] + rotate[i][1] * point[1] + rotate[i][2] * point[2] + offset[i] for i in range(3)]
    anchor = [-(rotate[0][j] * offset[0] + rotate[1][j] * offset[1] + rotate[2][j] * offset[2]) for j in range(3)]
    toward = [point[j] - anchor[j] for j in range(3)]
    length = jnp.sqrt(toward[0] * toward[0] + toward[1] * toward[1] + toward[2] * toward[2])
    ux, uy, uz = (toward[0] / length, toward[1] / length, toward[2] / length)
    quat_norm = jnp.sqrt(raw[6] * raw[6] + raw[7] * raw[7] + raw[8] * raw[8] + raw[9] * raw[9])
    qw, qx, qy, qz = (raw[6] / quat_norm, raw[7] / quat_norm, raw[8] / quat_norm, raw[9] / quat_norm)
    spin = [[1.0 - 2.0 * (qy * qy + qz * qz), 2.0 * (qx * qy - qw * qz), 2.0 * (qx * qz + qw * qy)], [2.0 * (qx * qy + qw * qz), 1.0 - 2.0 * (qx * qx + qz * qz), 2.0 * (qy * qz - qw * qx)], [2.0 * (qx * qz - qw * qy), 2.0 * (qy * qz + qw * qx), 1.0 - 2.0 * (qx * qx + qy * qy)]]
    squares = [jnp.exp(2.0 * raw[3 + k]) for k in range(3)]
    cov_world = [[spin[i][0] * spin[j][0] * squares[0] + spin[i][1] * spin[j][1] * squares[1] + spin[i][2] * spin[j][2] * squares[2] for j in range(3)] for i in range(3)]
    half_way = matmul3(rotate, cov_world)
    view_cov = [[half_way[a][0] * rotate[b][0] + half_way[a][1] * rotate[b][1] + half_way[a][2] * rotate[b][2] for b in range(3)] for a in range(3)]
    inverse = 1.0 / viewed[2]
    j_main = FOCAL * inverse
    j_side_x = -FOCAL * viewed[0] * inverse * inverse
    j_side_y = -FOCAL * viewed[1] * inverse * inverse
    s_xx = j_main * j_main * view_cov[0][0] + 2.0 * j_main * j_side_x * view_cov[0][2] + j_side_x * j_side_x * view_cov[2][2] + 0.3
    s_xy = j_main * j_main * view_cov[0][1] + j_main * j_side_y * view_cov[0][2] + j_side_x * j_main * view_cov[1][2] + j_side_x * j_side_y * view_cov[2][2]
    s_yy = j_main * j_main * view_cov[1][1] + 2.0 * j_main * j_side_y * view_cov[1][2] + j_side_y * j_side_y * view_cov[2][2] + 0.3
    determinant = s_xx * s_yy - s_xy * s_xy
    conic_a = s_yy / determinant
    conic_b = -s_xy / determinant
    conic_c = s_xx / determinant
    screen_u = FOCAL * viewed[0] * inverse + 2048.0
    screen_v = FOCAL * viewed[1] * inverse + 1024.0
    opacity = jax.nn.sigmoid(raw[10])
    xx, yy, zz = (ux * ux, uy * uy, uz * uz)
    basis = [SH_ZERO + 0.0 * ux, -SH_ONE * uy, SH_ONE * uz, -SH_ONE * ux, SH_TWO[0] * ux * uy, SH_TWO[1] * uy * uz, SH_TWO[2] * (2.0 * zz - xx - yy), SH_TWO[3] * ux * uz, SH_TWO[4] * (xx - yy), SH_THREE[0] * uy * (3.0 * xx - yy), SH_THREE[1] * ux * uy * uz, SH_THREE[2] * uy * (4.0 * zz - xx - yy), SH_THREE[3] * uz * (2.0 * zz - 3.0 * xx - 3.0 * yy), SH_THREE[4] * ux * (4.0 * zz - xx - yy), SH_THREE[5] * uz * (xx - yy), SH_THREE[6] * ux * (xx - 3.0 * yy)]
    channels = []
    for channel in range(3):
        total = 0.5 + basis[0] * raw[11 + channel]
        for k in range(1, 16):
            total = total + basis[k] * raw[11 + 3 * k + channel]
        channels.append(total)
    return jnp.stack([screen_u, screen_v, conic_a, conic_b, conic_c, opacity, channels[0], channels[1], channels[2]])

def render_loss(records, chosen, places, live_counts, wanted):
    picked = records[:, chosen]
    pixel = jnp.arange(256, dtype=jnp.int32)
    pixel_x = (places % 256 * 16)[:, None] + (pixel % 16)[None, :]
    pixel_y = (places // 256 * 16)[:, None] + (pixel // 16)[None, :]
    pixel_x = pixel_x.astype(jnp.float32) + 0.5
    pixel_y = pixel_y.astype(jnp.float32) + 0.5
    delta_x = pixel_x[:, None, :] - picked[0][:, :, None]
    delta_y = pixel_y[:, None, :] - picked[1][:, :, None]
    quad = picked[2][:, :, None] * delta_x * delta_x + 2.0 * picked[3][:, :, None] * delta_x * delta_y + picked[4][:, :, None] * delta_y * delta_y
    entries = chosen.shape[1]
    live = (jnp.arange(entries, dtype=jnp.int32)[None, :] < live_counts[:, None]).astype(jnp.float32)
    alpha = picked[5][:, :, None] * jnp.exp(-0.5 * quad) * live[:, :, None]
    through = jnp.cumprod(1.0 - alpha, axis=1)
    before = jnp.concatenate([jnp.ones_like(through[:, :1]), through[:, :-1]], axis=1)
    weight = alpha * before
    shown = jnp.einsum('ctl,tlx->tcx', picked[6:9], weight, precision=lax.Precision.HIGHEST)
    return 0.5 * jnp.sum((shown - wanted) ** 2)

def reference(positions, log_scales, rotations, opacities, colors, cameras, targets, tile_ids, tile_counts, tile_lists, fetch_ids):
    params = jnp.concatenate([positions, log_scales, rotations, opacities[None, :], colors], axis=0)
    owners = N_CAM * N_TILE
    slots = owners * CAP
    requesters = PASSES * N_CAM * N_TILE
    offsets = (jnp.arange(owners, dtype=jnp.int32) * G_DEV).reshape(N_CAM, N_TILE, 1)
    global_ids = (fetch_ids + offsets).reshape(requesters, slots).astype(jnp.int32)
    chosen = tile_lists.reshape(requesters, TILES_DEV, tile_lists.shape[-1])
    places = tile_ids.reshape(requesters, TILES_DEV)
    live_counts = tile_counts.reshape(requesters, TILES_DEV)
    wanted = targets.reshape(requesters, TILES_DEV, 3, targets.shape[-1])
    views = jnp.broadcast_to(cameras[:, :, None, :], (PASSES, N_CAM, N_TILE, 6)).reshape(requesters, 6)

    def one_device(item):
        ids_here, list_here, place_here, count_here, goal_here, view_here = item
        raw = params[:, ids_here]

        def loss_of(values):
            return render_loss(project(values, view_here[:, None]), list_here, place_here, count_here, goal_here)
        return jax.grad(loss_of)(raw)
    slot_grads = lax.map(one_device, (global_ids, chosen, places, live_counts, wanted, views))
    flat_grads = jnp.moveaxis(slot_grads, 1, 0).reshape(params.shape[0], requesters * slots)
    total = jnp.zeros_like(params).at[:, global_ids.reshape(-1)].add(flat_grads)
    return (total[0:3], total[3:6], total[6:10], total[10], total[11:])
```

```python
import jax
import jax.numpy as jnp
from jax import lax
from jax.experimental import pallas as pl
from jax.experimental.pallas import tpu as pltpu
from jax.sharding import PartitionSpec as P

N_CAM, N_TILE, N_DEV = 4, 64, 256
ROWS = 3
LIST, PIX, BLK = 256, 256, 32
MESH = pl.DeviceIdType.MESH
F32, BF16 = jnp.float32, jnp.bfloat16

FOCAL = 4096.0
SH_ZERO = 0.28209479177387814
SH_ONE = 0.4886025119029199
SH_TWO = [
    1.0925484305920792,
    -1.0925484305920792,
    0.31539156525252005,
    -1.0925484305920792,
    0.5462742152960396,
]
SH_THREE = [
    -0.5900435899266435,
    2.890611442640554,
    -0.4570457994644658,
    0.3731763325901154,
    -0.4570457994644658,
    1.445305721320277,
    -0.5900435899266435,
]


def matmul3(left, right):
    return [
        [
            left[i][0] * right[0][j] + left[i][1] * right[1][j] + left[i][2] * right[2][j]
            for j in range(3)
        ]
        for i in range(3)
    ]


def view_of(cam_ref):
    lane = lax.broadcasted_iota(jnp.int32, (8, 128), 1)
    view = lane // 16
    values = []
    for k in range(6):
        value = jnp.zeros((8, 128), F32)
        for c in range(N_CAM):
            for p in range(2):
                value = jnp.where(view == c * 2 + p, cam_ref[p, c, k], value)
        values.append(value)
    cos_a, sin_a = jnp.cos(values[0]), jnp.sin(values[0])
    cos_b, sin_b = jnp.cos(values[1]), jnp.sin(values[1])
    cos_c, sin_c = jnp.cos(values[2]), jnp.sin(values[2])
    rotate = [
        [cos_c * cos_b, cos_c * sin_b * sin_a - sin_c * cos_a, cos_c * sin_b * cos_a + sin_c * sin_a],
        [sin_c * cos_b, sin_c * sin_b * sin_a + cos_c * cos_a, sin_c * sin_b * cos_a - cos_c * sin_a],
        [-sin_b, cos_b * sin_a, cos_b * cos_a],
    ]
    offset = [values[3], values[4], 6.0 + values[5]]
    anchor = [
        -(rotate[0][j] * offset[0] + rotate[1][j] * offset[1] + rotate[2][j] * offset[2])
        for j in range(3)
    ]
    return [rotate[i][j] for i in range(3) for j in range(3)] + offset + anchor


def project(raw, view):
    rotate = [view[0:3], view[3:6], view[6:9]]
    offset, anchor = view[9:12], view[12:15]
    point = raw[0:3]
    viewed = [
        rotate[i][0] * point[0] + rotate[i][1] * point[1] + rotate[i][2] * point[2] + offset[i]
        for i in range(3)
    ]
    toward = [point[j] - anchor[j] for j in range(3)]
    length = jnp.sqrt(toward[0] * toward[0] + toward[1] * toward[1] + toward[2] * toward[2])
    per_length = 1.0 / length
    ux, uy, uz = (toward[0] * per_length, toward[1] * per_length, toward[2] * per_length)
    quat_norm = jnp.sqrt(raw[6] * raw[6] + raw[7] * raw[7] + raw[8] * raw[8] + raw[9] * raw[9])
    per_norm = 1.0 / quat_norm
    qw, qx, qy, qz = (raw[6] * per_norm, raw[7] * per_norm, raw[8] * per_norm, raw[9] * per_norm)
    spin = [
        [1.0 - 2.0 * (qy * qy + qz * qz), 2.0 * (qx * qy - qw * qz), 2.0 * (qx * qz + qw * qy)],
        [2.0 * (qx * qy + qw * qz), 1.0 - 2.0 * (qx * qx + qz * qz), 2.0 * (qy * qz - qw * qx)],
        [2.0 * (qx * qz - qw * qy), 2.0 * (qy * qz + qw * qx), 1.0 - 2.0 * (qx * qx + qy * qy)],
    ]
    squares = [jnp.exp(2.0 * raw[3 + k]) for k in range(3)]
    turned = matmul3(rotate, spin)

    def covariance(a, b):
        return (
            turned[a][0] * turned[b][0] * squares[0]
            + turned[a][1] * turned[b][1] * squares[1]
            + turned[a][2] * turned[b][2] * squares[2]
        )

    c00, c01, c02 = covariance(0, 0), covariance(0, 1), covariance(0, 2)
    c11, c12, c22 = covariance(1, 1), covariance(1, 2), covariance(2, 2)
    inverse = 1.0 / viewed[2]
    j_main = FOCAL * inverse
    j_side_x = -j_main * viewed[0] * inverse
    j_side_y = -j_main * viewed[1] * inverse
    s_xx = j_main * j_main * c00 + 2.0 * j_main * j_side_x * c02 + j_side_x * j_side_x * c22 + 0.3
    s_xy = (
        j_main * j_main * c01
        + j_main * j_side_y * c02
        + j_side_x * j_main * c12
        + j_side_x * j_side_y * c22
    )
    s_yy = j_main * j_main * c11 + 2.0 * j_main * j_side_y * c12 + j_side_y * j_side_y * c22 + 0.3
    per_det = 1.0 / (s_xx * s_yy - s_xy * s_xy)
    conic_a = s_yy * per_det
    conic_b = -s_xy * per_det
    conic_c = s_xx * per_det
    screen_u = j_main * viewed[0] + 2048.0
    screen_v = j_main * viewed[1] + 1024.0
    opacity = 1.0 / (1.0 + jnp.exp(-raw[10]))
    xx, yy, zz = (ux * ux, uy * uy, uz * uz)
    basis = [
        None,
        -SH_ONE * uy,
        SH_ONE * uz,
        -SH_ONE * ux,
        SH_TWO[0] * ux * uy,
        SH_TWO[1] * uy * uz,
        SH_TWO[2] * (2.0 * zz - xx - yy),
        SH_TWO[3] * ux * uz,
        SH_TWO[4] * (xx - yy),
        SH_THREE[0] * uy * (3.0 * xx - yy),
        SH_THREE[1] * ux * uy * uz,
        SH_THREE[2] * uy * (4.0 * zz - xx - yy),
        SH_THREE[3] * uz * (2.0 * zz - 3.0 * xx - 3.0 * yy),
        SH_THREE[4] * ux * (4.0 * zz - xx - yy),
        SH_THREE[5] * uz * (xx - yy),
        SH_THREE[6] * ux * (xx - 3.0 * yy),
    ]
    channels = []
    for channel in range(3):
        total = 0.5 + SH_ZERO * raw[11 + channel]
        for k in range(1, 16):
            total = total + basis[k] * raw[11 + 3 * k + channel]
        channels.append(total)
    return [screen_u, screen_v, conic_a, conic_b, conic_c, opacity] + channels


def split(value):
    high = value.astype(BF16)
    rest = value - high.astype(F32)
    mid = rest.astype(BF16)
    low = (rest - mid.astype(F32)).astype(BF16)
    return high, mid, low


def pick(chooser, value):
    high, mid, low = split(value)
    return (
        jnp.dot(chooser, high, preferred_element_type=F32)
        + jnp.dot(chooser, mid, preferred_element_type=F32)
    ) + jnp.dot(chooser, low, preferred_element_type=F32)


def turn(value, lanes):
    lanes = lanes % 128
    return value if lanes == 0 else pltpu.roll(value, lanes, 1)


def expand(refs, chunk):
    lane = lax.broadcasted_iota(jnp.int32, (8, 128), 1)
    row = lax.broadcasted_iota(jnp.int32, (8, 128), 0)
    own = lane // 16 == row
    here = pl.ds(pl.multiple_of(chunk * 128, 128), 128)
    out = []
    for ref in refs:
        for k in range(ref.shape[0]):
            value = jnp.where(own, jnp.broadcast_to(ref[k : k + 1, here], (8, 128)), 0.0)
            for step in (16, 32, 64):
                value = value + pltpu.roll(value, step, 1)
            out.append(value)
    return out


def project_kernel(pos, scl, rot, opa, col, cam, out, view_ref):
    for k, value in enumerate(view_of(cam)):
        view_ref[k] = value

    def step(chunk, carry):
        view = [view_ref[k] for k in range(15)]
        record = project(expand((pos, scl, rot, opa, col), chunk), view)
        group = lax.broadcasted_iota(jnp.int32, (8, 128), 1) // 32
        rows = pl.ds(pl.multiple_of(chunk * 8, 8), 8)
        for c in range(N_CAM):
            for m in range(ROWS):
                value = jnp.zeros((8, 128), F32)
                for q in range(4):
                    if 4 * m + q < 9:
                        value = jnp.where(group == q, turn(record[4 * m + q], (q - c) * 32), value)
                out[c * ROWS + m, rows, :] = value
        return carry

    lax.fori_loop(0, 8, step, 0)


def place():
    return lax.axis_index("cam"), lax.axis_index("tile")


def across(c, t, i):
    index = lax.rem(c * 4 + t // 16 + i, 16)
    return (index // 4, lax.rem(index, 4) * 16 + lax.rem(t, 16))


def along(c, t, i):
    return (c, (t // 16) * 16 + lax.rem(lax.rem(t, 16) + i, 16))


def greet(c, t):
    barrier = pltpu.get_barrier_semaphore()

    def hail(i, carry):
        pl.semaphore_signal(barrier, inc=1, device_id=along(c, t, i), device_id_type=MESH)
        pl.semaphore_signal(barrier, inc=1, device_id=across(c, t, i), device_id_type=MESH)
        return carry

    lax.fori_loop(1, 16, hail, 0)
    pl.semaphore_wait(barrier, 30)


def exchange(src, dst, c, t, send, recv, own):
    me = c * N_TILE + t
    local = pltpu.make_async_copy(src.at[me], dst.at[me], own)
    local.start()

    def one(i, carry):
        to = lax.rem(me + i, N_DEV)
        pltpu.make_async_remote_copy(
            src_ref=src.at[to],
            dst_ref=dst.at[me],
            send_sem=send,
            recv_sem=recv,
            device_id=(to // N_TILE, lax.rem(to, N_TILE)),
            device_id_type=MESH,
        ).start()
        return carry

    lax.fori_loop(1, N_DEV, one, 0, unroll=5)
    most = pl.ds(0, N_DEV - 1)
    pltpu.make_async_copy(src.at[most], src.at[most], send).wait()
    pltpu.make_async_copy(dst.at[most], dst.at[most], recv).wait()
    local.wait()


def forward_kernel(mine, records, table, out, packed, send_a, recv_a, own_a, send_b, recv_b, send_c, recv_c, own_c):
    c, t = place()
    me = c * N_TILE + t
    greet(c, t)
    local = pltpu.make_async_copy(mine.at[0], table.at[me], own_a)
    local.start()

    def first(i, carry):
        pltpu.make_async_remote_copy(
            src_ref=mine.at[0],
            dst_ref=table.at[me],
            send_sem=send_a,
            recv_sem=recv_a,
            device_id=along(c, t, i),
            device_id_type=MESH,
        ).start()
        return carry

    lax.fori_loop(1, 16, first, 0)
    local.wait()
    some = pl.ds(0, 15)
    pltpu.make_async_copy(table.at[some], table.at[some], send_a).wait()
    pltpu.make_async_copy(table.at[some], table.at[some], recv_a).wait()
    line = pl.ds(c * N_TILE + (t // 16) * 16, 16)

    def second(i, carry):
        pltpu.make_async_remote_copy(
            src_ref=table.at[line],
            dst_ref=table.at[line],
            send_sem=send_b,
            recv_sem=recv_b,
            device_id=across(c, t, i),
            device_id_type=MESH,
        ).start()
        return carry

    lax.fori_loop(1, 16, second, 0)
    most = pl.ds(0, 240)
    pltpu.make_async_copy(table.at[most], table.at[most], send_b).wait()
    pltpu.make_async_copy(table.at[most], table.at[most], recv_b).wait()

    lane = lax.broadcasted_iota(jnp.int32, (64, 128), 1)
    even = lax.rem(lane // 16, 2) == 0
    for g in range(N_CAM):
        wanted = table[g * N_TILE : (g + 1) * N_TILE, 0, :]
        chooser = jnp.where(wanted == lax.rem(lane, 64), 1.0, 0.0).astype(BF16)
        for m in range(ROWS):
            value = records[g * ROWS + m]
            both = jnp.concatenate([jnp.where(even, value, 0.0), jnp.where(even, 0.0, value)], axis=0)
            packed[g * N_TILE : (g + 1) * N_TILE, m, :] = pick(chooser, both)
    exchange(packed, out, c, t, send_c, recv_c, own_c)


def backward_kernel(grads, out, ready, send, recv, own):
    c, t = place()
    greet(c, t)

    def hail(i, carry):
        pl.semaphore_signal(ready, inc=1, device_id=across(c, t, i), device_id_type=MESH)
        return carry

    lax.fori_loop(1, 16, hail, 0)
    pl.semaphore_wait(ready, 15)
    exchange(grads, out, c, t, send, recv, own)


def render_kernel(place_ref, count_ref, data, fetch, list_col, list_row, target, out, cols, alpha_ref, through_ref, lost):
    lane = lax.broadcasted_iota(jnp.int32, (LIST, 128), 1)
    lane_b = lax.broadcasted_iota(jnp.int32, (BLK, 128), 1)
    row_b = lax.broadcasted_iota(jnp.int32, (BLK, 128), 0)
    lane_1 = lax.broadcasted_iota(jnp.int32, (1, 128), 1)
    parts = split(jnp.concatenate([data[:, m, :] for m in range(ROWS)], axis=1))
    blocks = LIST // BLK
    total = None
    for p in range(2):
        slot = list_col[p]
        owner = slot // 8
        spot = lax.rem(slot, 8)
        wide = lax.broadcasted_iota(jnp.int32, (LIST, N_DEV), 1)
        chooser = jnp.where(wide == owner, 1.0, 0.0).astype(BF16)
        within = lax.rem(fetch[p], 16).astype(F32).astype(BF16)
        near = jnp.dot(chooser, within, preferred_element_type=F32)
        eight = lax.broadcasted_iota(jnp.int32, near.shape, 1)
        column = jnp.sum(jnp.where(eight == spot, near, 0.0), axis=1, keepdims=True)
        live_lane = (lax.rem(lane // 16, 2) == p) & (lax.rem(lane, 16).astype(F32) == column)
        picked = jnp.dot(chooser, parts[0], preferred_element_type=F32)
        picked = picked + jnp.dot(chooser, parts[1], preferred_element_type=F32)
        picked = picked + jnp.dot(chooser, parts[2], preferred_element_type=F32)
        for v in range(9):
            m, q = v // 4, v % 4
            value = jnp.where(live_lane & (lane // 32 == q), picked[:, m * 128 : (m + 1) * 128], 0.0)
            cols[v] = jnp.broadcast_to(jnp.sum(value, axis=1, keepdims=True), (LIST, 128))
        cols[9] = jnp.where(live_lane, 1.0, 0.0)

        tile = place_ref[p]
        count = count_ref[p]
        left = (lax.rem(tile, 256) * 16).astype(F32) + 0.5
        top = ((tile // 256) * 16).astype(F32) + 0.5
        px = left + lax.rem(lane_1, 16).astype(F32)
        py = [top + ((lane_1 + h * 128) // 16).astype(F32) for h in range(2)]

        def ahead(b, carry):
            rows = pl.ds(pl.multiple_of(b * BLK, BLK), BLK)
            u, v, ca, cb, cc, o = [cols[k, rows, :] for k in range(6)]
            shade = [cols[k, rows, :] for k in (6, 7, 8)]
            live = row_b + b * BLK < count
            dx = px - u
            dxx = ca * dx * dx
            result = []
            for h in range(2):
                passed, shown = carry[h][0], carry[h][1:]
                dy = py[h] - v
                quad = dxx + 2.0 * cb * dx * dy + cc * dy * dy
                alpha = jnp.where(live, o * jnp.exp(-0.5 * quad), 0.0)
                run = 1.0 - alpha
                for s in (1, 2, 4, 8, 16):
                    run = run * jnp.where(row_b >= s, pltpu.roll(run, s, 0), 1.0)
                before = passed * jnp.where(row_b >= 1, pltpu.roll(run, 1, 0), 1.0)
                weight = alpha * before
                alpha_ref[h, rows, :] = alpha
                through_ref[h, rows, :] = before
                result.append(
                    (passed * run[BLK - 1 : BLK, :],)
                    + tuple(s + jnp.sum(k * weight, axis=0, keepdims=True) for s, k in zip(shown, shade))
                )
            return tuple(result)

        one, zero = jnp.ones((1, 128), F32), jnp.zeros((1, 128), F32)
        shown = lax.fori_loop(0, blocks, ahead, ((one, zero, zero, zero),) * 2)
        miss = [
            [shown[h][1 + k] - target[p, k : k + 1, h * 128 : (h + 1) * 128] for k in range(3)]
            for h in range(2)
        ]

        def back(i, carry):
            b = blocks - 1 - i
            rows = pl.ds(pl.multiple_of(b * BLK, BLK), BLK)
            u, v, ca, cb, cc, o = [cols[k, rows, :] for k in range(6)]
            shade = [cols[k, rows, :] for k in (6, 7, 8)]
            dx = px - u
            sums = [0.0] * 9
            result = []
            for h in range(2):
                alpha, before = alpha_ref[h, rows, :], through_ref[h, rows, :]
                dy = py[h] - v
                weight = alpha * before
                pull = shade[0] * miss[h][0] + shade[1] * miss[h][1] + shade[2] * miss[h][2]
                run = pull * weight
                for s in (1, 2, 4, 8, 16):
                    run = run + jnp.where(row_b < BLK - s, pltpu.roll(run, BLK - s, 0), 0.0)
                after = carry[h] + jnp.where(row_b < BLK - 1, pltpu.roll(run, BLK - 1, 0), 0.0)
                result.append(carry[h] + run[0:1, :])
                slope = (before * pull - after / (1.0 - alpha)) * alpha
                tilt_x, tilt_y = slope * dx, slope * dy
                terms = [tilt_x, tilt_y, tilt_x * dx, tilt_x * dy, tilt_y * dy, slope]
                terms = terms + [weight * miss[h][k] for k in range(3)]
                sums = [a + t for a, t in zip(sums, terms)]
            m_x, m_y, m_xx, m_xy, m_yy, m_0, *g_shade = [jnp.sum(s, axis=1, keepdims=True) for s in sums]
            grads = [
                ca * m_x + cb * m_y,
                cb * m_x + cc * m_y,
                -0.5 * m_xx,
                -m_xy,
                -0.5 * m_yy,
                m_0 / o,
            ] + g_shade
            keep = cols[9, rows, :]
            for m in range(ROWS):
                value = jnp.zeros((BLK, 128), F32)
                for q in range(4):
                    if 4 * m + q < 9:
                        value = jnp.where(lane_b // 32 == q, jnp.broadcast_to(grads[4 * m + q], (BLK, 128)), value)
                lost[rows, m * 128 : (m + 1) * 128] = value * keep
            return tuple(result)

        lax.fori_loop(0, blocks, back, (zero, zero))
        tall = lax.broadcasted_iota(jnp.int32, (N_DEV, LIST), 0)
        giver = jnp.where(tall == list_row[p] // 8, 1.0, 0.0).astype(BF16)
        part = pick(giver, lost[...])
        total = part if total is None else total + part
    for m in range(ROWS):
        out[:, m, :] = total[:, m * 128 : (m + 1) * 128]


def gradient_kernel(pos, scl, rot, opa, col, cam, table, arrived, g_pos, g_scl, g_rot, g_opa, g_col, view_ref, cot):
    for k, value in enumerate(view_of(cam)):
        view_ref[k] = value
    lane = lax.broadcasted_iota(jnp.int32, (64, 128), 1)
    even = lax.rem(lane // 16, 2) == 0
    for g in range(N_CAM):
        wanted = table[g * N_TILE : (g + 1) * N_TILE, 0, :]
        chooser = jnp.where(wanted == lax.rem(lane, 64), 1.0, 0.0).T.astype(BF16)
        for m in range(ROWS):
            both = pick(chooser, arrived[g * N_TILE : (g + 1) * N_TILE, m, :])
            value = jnp.where(even, both[0:64], both[64:128])
            for q in range(4):
                v = 4 * m + q
                if v < 9:
                    turned = turn(value, (g - q) * 32)
                    if g == 0:
                        cot[v] = turned
                    else:
                        cot[v] = jnp.where(lane // 32 == g, turned, cot[v])
    own_lane = lax.broadcasted_iota(jnp.int32, (8, 128), 1) // 16
    own = own_lane == lax.broadcasted_iota(jnp.int32, (8, 128), 0)

    def step(chunk, carry):
        view = [view_ref[k] for k in range(15)]
        raw = expand((pos, scl, rot, opa, col), chunk)
        rows = pl.ds(pl.multiple_of(chunk * 8, 8), 8)
        here = pl.ds(pl.multiple_of(chunk * 128, 128), 128)
        _, pull = jax.vjp(lambda values: project(values, view), raw)
        (grads,) = pull([cot[v, rows, :] for v in range(9)])
        k = 0
        for ref in (g_pos, g_scl, g_rot, g_opa, g_col):
            for r in range(ref.shape[0]):
                value = grads[k]
                for s in (16, 32, 64):
                    value = value + pltpu.roll(value, s, 1)
                ref[r : r + 1, here] = jnp.sum(jnp.where(own, value, 0.0), axis=0, keepdims=True)
                k += 1
        return carry

    lax.fori_loop(0, 8, step, 0)


VMEM = pl.BlockSpec(memory_space=pltpu.VMEM)
SMEM = pl.BlockSpec(memory_space=pltpu.SMEM)
DMA = pltpu.SemaphoreType.DMA


def shape(*dims, dtype=F32):
    return jax.ShapeDtypeStruct(dims, dtype)


def body(
    positions,
    log_scales,
    rotations,
    opacities,
    colors,
    cameras,
    targets,
    tile_ids,
    tile_counts,
    tile_lists,
    fetch_ids,
):
    params = (positions, log_scales, rotations, opacities.reshape(1, 1024), colors)
    records = pl.pallas_call(
        project_kernel,
        out_shape=shape(12, 64, 128),
        in_specs=[VMEM] * 5 + [SMEM],
        out_specs=VMEM,
        scratch_shapes=[pltpu.VMEM((15, 8, 128), F32)],
    )(*params, cameras)

    fetched = fetch_ids.reshape(2, N_DEV, 8)
    block = fetched[:, 0, 0] // 16
    mine = jnp.repeat(block, 64).reshape(1, 1, 128)
    table, data = pl.pallas_call(
        forward_kernel,
        out_shape=(shape(N_DEV, 1, 128, dtype=jnp.int32), shape(N_DEV, ROWS, 128)),
        in_specs=[VMEM] * 2,
        out_specs=(VMEM, VMEM),
        scratch_shapes=[pltpu.VMEM((N_DEV, ROWS, 128), F32)] + [DMA] * 8,
        compiler_params=pltpu.CompilerParams(collective_id=0, has_side_effects=True),
    )(mine, records)

    lists = tile_lists.reshape(2, LIST)
    record_grads = pl.pallas_call(
        render_kernel,
        out_shape=shape(N_DEV, ROWS, 128),
        in_specs=[SMEM] * 2 + [VMEM] * 5,
        out_specs=VMEM,
        scratch_shapes=[
            pltpu.VMEM((10, LIST, 128), F32),
            pltpu.VMEM((2, LIST, 128), F32),
            pltpu.VMEM((2, LIST, 128), F32),
            pltpu.VMEM((LIST, 3 * 128), F32),
        ],
    )(
        tile_ids.reshape(2),
        tile_counts.reshape(2),
        data,
        fetched,
        lists.reshape(2, LIST, 1),
        lists.reshape(2, 1, LIST),
        targets.reshape(2, 3, PIX),
    )

    returned = pl.pallas_call(
        backward_kernel,
        out_shape=shape(N_DEV, ROWS, 128),
        in_specs=[VMEM],
        out_specs=VMEM,
        scratch_shapes=[pltpu.SemaphoreType.REGULAR] + [DMA] * 3,
        compiler_params=pltpu.CompilerParams(collective_id=1, has_side_effects=True),
    )(record_grads)

    g_pos, g_scl, g_rot, g_opa, g_col = pl.pallas_call(
        gradient_kernel,
        out_shape=tuple(shape(n, 1024) for n in (3, 3, 4, 1, 48)),
        in_specs=[VMEM] * 5 + [SMEM] + [VMEM] * 2,
        out_specs=(VMEM,) * 5,
        scratch_shapes=[pltpu.VMEM((15, 8, 128), F32), pltpu.VMEM((9, 64, 128), F32)],
    )(*params, cameras, table, returned)
    return g_pos, g_scl, g_rot, g_opa.reshape(1024), g_col


def solution(mesh):
    return jax.shard_map(
        body,
        mesh=mesh,
        in_specs=(
            P(None, ("cam", "tile")),
            P(None, ("cam", "tile")),
            P(None, ("cam", "tile")),
            P(("cam", "tile")),
            P(None, ("cam", "tile")),
            P(),
            P(None, "cam", "tile", None, None),
            P(None, "cam", "tile"),
            P(None, "cam", "tile"),
            P(None, "cam", "tile", None),
            P(None, "cam", "tile", None, None, None),
        ),
        out_specs=(
            P(None, ("cam", "tile")),
            P(None, ("cam", "tile")),
            P(None, ("cam", "tile")),
            P(("cam", "tile")),
            P(None, ("cam", "tile")),
        ),
        check_vma=False,
    )
```

```python
import jax
import jax.numpy as jnp
from jax import lax
from jax.experimental import pallas as pl
from jax.experimental.pallas import tpu as pltpu
from jax.sharding import PartitionSpec as P

N_CAM, N_TILE, N_DEV = 4, 64, 256
ROWS = 3
LIST, PIX, BLK = 256, 256, 32
MESH = pl.DeviceIdType.MESH
F32, BF16 = jnp.float32, jnp.bfloat16

FOCAL = 4096.0
SH_ZERO = 0.28209479177387814
SH_ONE = 0.4886025119029199
SH_TWO = [
    1.0925484305920792,
    -1.0925484305920792,
    0.31539156525252005,
    -1.0925484305920792,
    0.5462742152960396,
]
SH_THREE = [
    -0.5900435899266435,
    2.890611442640554,
    -0.4570457994644658,
    0.3731763325901154,
    -0.4570457994644658,
    1.445305721320277,
    -0.5900435899266435,
]


def matmul3(left, right):
    return [
        [
            left[i][0] * right[0][j] + left[i][1] * right[1][j] + left[i][2] * right[2][j]
            for j in range(3)
        ]
        for i in range(3)
    ]


def view_of(cam_ref):
    lane = lax.broadcasted_iota(jnp.int32, (8, 128), 1)
    view = lane // 16
    values = []
    for k in range(6):
        value = jnp.zeros((8, 128), F32)
        for c in range(N_CAM):
            for p in range(2):
                value = jnp.where(view == c * 2 + p, cam_ref[p, c, k], value)
        values.append(value)
    cos_a, sin_a = jnp.cos(values[0]), jnp.sin(values[0])
    cos_b, sin_b = jnp.cos(values[1]), jnp.sin(values[1])
    cos_c, sin_c = jnp.cos(values[2]), jnp.sin(values[2])
    rotate = [
        [cos_c * cos_b, cos_c * sin_b * sin_a - sin_c * cos_a, cos_c * sin_b * cos_a + sin_c * sin_a],
        [sin_c * cos_b, sin_c * sin_b * sin_a + cos_c * cos_a, sin_c * sin_b * cos_a - cos_c * sin_a],
        [-sin_b, cos_b * sin_a, cos_b * cos_a],
    ]
    offset = [values[3], values[4], 6.0 + values[5]]
    anchor = [
        -(rotate[0][j] * offset[0] + rotate[1][j] * offset[1] + rotate[2][j] * offset[2])
        for j in range(3)
    ]
    return [rotate[i][j] for i in range(3) for j in range(3)] + offset + anchor


def project(raw, view):
    rotate = [view[0:3], view[3:6], view[6:9]]
    offset, anchor = view[9:12], view[12:15]
    point = raw[0:3]
    viewed = [
        rotate[i][0] * point[0] + rotate[i][1] * point[1] + rotate[i][2] * point[2] + offset[i]
        for i in range(3)
    ]
    toward = [point[j] - anchor[j] for j in range(3)]
    length = jnp.sqrt(toward[0] * toward[0] + toward[1] * toward[1] + toward[2] * toward[2])
    per_length = 1.0 / length
    ux, uy, uz = (toward[0] * per_length, toward[1] * per_length, toward[2] * per_length)
    quat_norm = jnp.sqrt(raw[6] * raw[6] + raw[7] * raw[7] + raw[8] * raw[8] + raw[9] * raw[9])
    per_norm = 1.0 / quat_norm
    qw, qx, qy, qz = (raw[6] * per_norm, raw[7] * per_norm, raw[8] * per_norm, raw[9] * per_norm)
    spin = [
        [1.0 - 2.0 * (qy * qy + qz * qz), 2.0 * (qx * qy - qw * qz), 2.0 * (qx * qz + qw * qy)],
        [2.0 * (qx * qy + qw * qz), 1.0 - 2.0 * (qx * qx + qz * qz), 2.0 * (qy * qz - qw * qx)],
        [2.0 * (qx * qz - qw * qy), 2.0 * (qy * qz + qw * qx), 1.0 - 2.0 * (qx * qx + qy * qy)],
    ]
    squares = [jnp.exp(2.0 * raw[3 + k]) for k in range(3)]
    turned = matmul3(rotate, spin)

    def covariance(a, b):
        return (
            turned[a][0] * turned[b][0] * squares[0]
            + turned[a][1] * turned[b][1] * squares[1]
            + turned[a][2] * turned[b][2] * squares[2]
        )

    c00, c01, c02 = covariance(0, 0), covariance(0, 1), covariance(0, 2)
    c11, c12, c22 = covariance(1, 1), covariance(1, 2), covariance(2, 2)
    inverse = 1.0 / viewed[2]
    j_main = FOCAL * inverse
    j_side_x = -j_main * viewed[0] * inverse
    j_side_y = -j_main * viewed[1] * inverse
    s_xx = j_main * j_main * c00 + 2.0 * j_main * j_side_x * c02 + j_side_x * j_side_x * c22 + 0.3
    s_xy = (
        j_main * j_main * c01
        + j_main * j_side_y * c02
        + j_side_x * j_main * c12
        + j_side_x * j_side_y * c22
    )
    s_yy = j_main * j_main * c11 + 2.0 * j_main * j_side_y * c12 + j_side_y * j_side_y * c22 + 0.3
    per_det = 1.0 / (s_xx * s_yy - s_xy * s_xy)
    conic_a = s_yy * per_det
    conic_b = -s_xy * per_det
    conic_c = s_xx * per_det
    screen_u = j_main * viewed[0] + 2048.0
    screen_v = j_main * viewed[1] + 1024.0
    opacity = 1.0 / (1.0 + jnp.exp(-raw[10]))
    xx, yy, zz = (ux * ux, uy * uy, uz * uz)
    basis = [
        None,
        -SH_ONE * uy,
        SH_ONE * uz,
        -SH_ONE * ux,
        SH_TWO[0] * ux * uy,
        SH_TWO[1] * uy * uz,
        SH_TWO[2] * (2.0 * zz - xx - yy),
        SH_TWO[3] * ux * uz,
        SH_TWO[4] * (xx - yy),
        SH_THREE[0] * uy * (3.0 * xx - yy),
        SH_THREE[1] * ux * uy * uz,
        SH_THREE[2] * uy * (4.0 * zz - xx - yy),
        SH_THREE[3] * uz * (2.0 * zz - 3.0 * xx - 3.0 * yy),
        SH_THREE[4] * ux * (4.0 * zz - xx - yy),
        SH_THREE[5] * uz * (xx - yy),
        SH_THREE[6] * ux * (xx - 3.0 * yy),
    ]
    channels = []
    for channel in range(3):
        total = 0.5 + SH_ZERO * raw[11 + channel]
        for k in range(1, 16):
            total = total + basis[k] * raw[11 + 3 * k + channel]
        channels.append(total)
    return [screen_u, screen_v, conic_a, conic_b, conic_c, opacity] + channels


def split(value):
    high = value.astype(BF16)
    rest = value - high.astype(F32)
    mid = rest.astype(BF16)
    low = (rest - mid.astype(F32)).astype(BF16)
    return high, mid, low


def pick(chooser, value):
    high, mid, low = split(value)
    return (
        jnp.dot(chooser, high, preferred_element_type=F32)
        + jnp.dot(chooser, mid, preferred_element_type=F32)
    ) + jnp.dot(chooser, low, preferred_element_type=F32)


def turn(value, lanes):
    lanes = lanes % 128
    return value if lanes == 0 else pltpu.roll(value, lanes, 1)


def spread_of(first):
    lane = lax.broadcasted_iota(jnp.int32, (128, 256), 1)
    row = lax.broadcasted_iota(jnp.int32, (128, 256), 0)
    return jnp.where(row == (first + lane // 128) * 16 + lax.rem(lane, 16), 1.0, 0.0).astype(BF16)


def expand(refs, flat, wide):
    flat[56:64, :] = jnp.zeros((8, 1024), F32)
    start = 0
    for ref in refs:
        flat[start : start + ref.shape[0], :] = ref[...]
        start += ref.shape[0]
    parts = split(jnp.concatenate([flat[:, j * 128 : (j + 1) * 128] for j in range(8)], axis=0))
    for i in range(0, 8, 2):
        spread = spread_of(i)
        value = (
            jnp.dot(parts[0], spread, preferred_element_type=F32)
            + jnp.dot(parts[1], spread, preferred_element_type=F32)
        ) + jnp.dot(parts[2], spread, preferred_element_type=F32)
        wide[:, i, :] = value[:, 0:128]
        wide[:, i + 1, :] = value[:, 128:256]


def project_chunk(chunk, wide, view_ref, out):
    view = [view_ref[k] for k in range(15)]
    record = project([wide[chunk * 64 + k] for k in range(59)], view)
    group = lax.broadcasted_iota(jnp.int32, (8, 128), 1) // 32
    rows = pl.ds(pl.multiple_of(chunk * 8, 8), 8)
    for c in range(N_CAM):
        for m in range(ROWS):
            value = jnp.zeros((8, 128), F32)
            for q in range(4):
                if 4 * m + q < 9:
                    value = jnp.where(group == q, turn(record[4 * m + q], (q - c) * 32), value)
            out[c * ROWS + m, rows, :] = value


def place():
    return lax.axis_index("cam"), lax.axis_index("tile")


def across(c, t, i):
    index = lax.rem(c * 4 + t // 16 + i, 16)
    return (index // 4, lax.rem(index, 4) * 16 + lax.rem(t, 16))


def along(c, t, i):
    return (c, (t // 16) * 16 + lax.rem(lax.rem(t, 16) + i, 16))


def greet(c, t):
    barrier = pltpu.get_barrier_semaphore()

    def hail(i, carry):
        pl.semaphore_signal(barrier, inc=1, device_id=along(c, t, i), device_id_type=MESH)
        pl.semaphore_signal(barrier, inc=1, device_id=across(c, t, i), device_id_type=MESH)
        return carry

    lax.fori_loop(1, 16, hail, 0)
    return barrier


def send_rows(src, dst, c, t, send, recv, low, high):
    me = c * N_TILE + t

    def one(i, carry):
        to = lax.rem(me + i, N_DEV)
        pltpu.make_async_remote_copy(
            src_ref=src.at[to],
            dst_ref=dst.at[me],
            send_sem=send,
            recv_sem=recv,
            device_id=(to // N_TILE, lax.rem(to, N_TILE)),
            device_id_type=MESH,
        ).start()
        return carry

    lax.fori_loop(low, high, one, 0, unroll=5)


def wait_rows(src, dst, send, recv):
    most = pl.ds(0, N_DEV - 1)
    pltpu.make_async_copy(src.at[most], src.at[most], send).wait()
    pltpu.make_async_copy(dst.at[most], dst.at[most], recv).wait()


def main_kernel(
    place_ref,
    count_ref,
    cam,
    pos,
    scl,
    rot,
    opa,
    col,
    mine,
    fetch,
    list_col,
    list_row,
    target,
    table,
    returned,
    flat,
    wide,
    view_ref,
    records,
    packed,
    data,
    grads,
    cols,
    alpha_ref,
    through_ref,
    lost,
    send_a,
    recv_a,
    own_a,
    send_b,
    recv_b,
    send_c,
    recv_c,
    own_c,
    send_d,
    recv_d,
    own_d,
):
    c, t = place()
    me = c * N_TILE + t
    barrier = greet(c, t)
    local = pltpu.make_async_copy(mine.at[0], table.at[me], own_a)
    local.start()
    for k, value in enumerate(view_of(cam)):
        view_ref[k] = value
    expand((pos, scl, rot, opa, col), flat, wide)

    def step(chunk, carry):
        project_chunk(chunk, wide, view_ref, records)
        return carry

    pl.semaphore_wait(barrier, 30)

    def first(i, carry):
        pltpu.make_async_remote_copy(
            src_ref=mine.at[0],
            dst_ref=table.at[me],
            send_sem=send_a,
            recv_sem=recv_a,
            device_id=along(c, t, i),
            device_id_type=MESH,
        ).start()
        return carry

    lax.fori_loop(1, 16, first, 0)
    lax.fori_loop(0, 4, step, 0)
    local.wait()
    some = pl.ds(0, 15)
    pltpu.make_async_copy(table.at[some], table.at[some], send_a).wait()
    pltpu.make_async_copy(table.at[some], table.at[some], recv_a).wait()
    line = pl.ds(c * N_TILE + (t // 16) * 16, 16)

    def second(i, carry):
        pltpu.make_async_remote_copy(
            src_ref=table.at[line],
            dst_ref=table.at[line],
            send_sem=send_b,
            recv_sem=recv_b,
            device_id=across(c, t, i),
            device_id_type=MESH,
        ).start()
        return carry

    lax.fori_loop(1, 16, second, 0)
    lax.fori_loop(4, 8, step, 0)
    most = pl.ds(0, 240)
    pltpu.make_async_copy(table.at[most], table.at[most], send_b).wait()
    pltpu.make_async_copy(table.at[most], table.at[most], recv_b).wait()

    lane = lax.broadcasted_iota(jnp.int32, (64, 128), 1)
    even = lax.rem(lane // 16, 2) == 0
    for g in range(N_CAM):
        wanted = table[g * N_TILE : (g + 1) * N_TILE, 0, :]
        chooser = jnp.where(wanted == lax.rem(lane, 64), 1.0, 0.0).astype(BF16)
        for m in range(ROWS):
            value = records[g * ROWS + m]
            both = jnp.concatenate([jnp.where(even, value, 0.0), jnp.where(even, 0.0, value)], axis=0)
            packed[g * N_TILE : (g + 1) * N_TILE, m, :] = pick(chooser, both)
    local = pltpu.make_async_copy(packed.at[me], data.at[me], own_c)
    local.start()
    send_rows(packed, data, c, t, send_c, recv_c, 1, N_DEV)
    local.wait()
    wait_rows(packed, data, send_c, recv_c)
    render(place_ref, count_ref, data, fetch, list_col, list_row, target, grads, cols, alpha_ref, through_ref, lost)
    local = pltpu.make_async_copy(grads.at[me], returned.at[me], own_d)
    local.start()
    send_rows(grads, returned, c, t, send_d, recv_d, 1, N_DEV)
    local.wait()
    wait_rows(grads, returned, send_d, recv_d)


def render(place_ref, count_ref, data, fetch, list_col, list_row, target, out, cols, alpha_ref, through_ref, lost):
    lane = lax.broadcasted_iota(jnp.int32, (LIST, 128), 1)
    lane_b = lax.broadcasted_iota(jnp.int32, (BLK, 128), 1)
    row_b = lax.broadcasted_iota(jnp.int32, (BLK, 128), 0)
    lane_1 = lax.broadcasted_iota(jnp.int32, (1, 128), 1)
    parts = split(jnp.concatenate([data[:, m, :] for m in range(ROWS)], axis=1))
    blocks = LIST // BLK
    total = None
    for p in range(2):
        slot = list_col[p]
        owner = slot // 8
        spot = lax.rem(slot, 8)
        wide = lax.broadcasted_iota(jnp.int32, (LIST, N_DEV), 1)
        chooser = jnp.where(wide == owner, 1.0, 0.0).astype(BF16)
        within = lax.rem(fetch[p], 16).astype(F32).astype(BF16)
        near = jnp.dot(chooser, within, preferred_element_type=F32)
        eight = lax.broadcasted_iota(jnp.int32, near.shape, 1)
        column = jnp.sum(jnp.where(eight == spot, near, 0.0), axis=1, keepdims=True)
        live_lane = (lax.rem(lane // 16, 2) == p) & (lax.rem(lane, 16).astype(F32) == column)
        picked = jnp.dot(chooser, parts[0], preferred_element_type=F32)
        picked = picked + jnp.dot(chooser, parts[1], preferred_element_type=F32)
        picked = picked + jnp.dot(chooser, parts[2], preferred_element_type=F32)
        for v in range(9):
            m, q = v // 4, v % 4
            value = jnp.where(live_lane & (lane // 32 == q), picked[:, m * 128 : (m + 1) * 128], 0.0)
            cols[v] = jnp.broadcast_to(jnp.sum(value, axis=1, keepdims=True), (LIST, 128))
        cols[9] = jnp.where(live_lane, 1.0, 0.0)

        tile = place_ref[p]
        count = count_ref[p]
        left = (lax.rem(tile, 256) * 16).astype(F32) + 0.5
        top = ((tile // 256) * 16).astype(F32) + 0.5
        px = left + lax.rem(lane_1, 16).astype(F32)
        py = [top + ((lane_1 + h * 128) // 16).astype(F32) for h in range(2)]

        def ahead(b, carry):
            rows = pl.ds(pl.multiple_of(b * BLK, BLK), BLK)
            u, v, ca, cb, cc, o = [cols[k, rows, :] for k in range(6)]
            shade = [cols[k, rows, :] for k in (6, 7, 8)]
            live = row_b + b * BLK < count
            dx = px - u
            dxx = ca * dx * dx
            result = []
            for h in range(2):
                passed, shown = carry[h][0], carry[h][1:]
                dy = py[h] - v
                quad = dxx + 2.0 * cb * dx * dy + cc * dy * dy
                alpha = jnp.where(live, o * jnp.exp(-0.5 * quad), 0.0)
                run = 1.0 - alpha
                for s in (1, 2, 4, 8, 16):
                    run = run * jnp.where(row_b >= s, pltpu.roll(run, s, 0), 1.0)
                before = passed * jnp.where(row_b >= 1, pltpu.roll(run, 1, 0), 1.0)
                weight = alpha * before
                alpha_ref[h, rows, :] = alpha
                through_ref[h, rows, :] = before
                result.append(
                    (passed * run[BLK - 1 : BLK, :],)
                    + tuple(s + jnp.sum(k * weight, axis=0, keepdims=True) for s, k in zip(shown, shade))
                )
            return tuple(result)

        one, zero = jnp.ones((1, 128), F32), jnp.zeros((1, 128), F32)
        shown = lax.fori_loop(0, blocks, ahead, ((one, zero, zero, zero),) * 2)
        miss = [
            [shown[h][1 + k] - target[p, k : k + 1, h * 128 : (h + 1) * 128] for k in range(3)]
            for h in range(2)
        ]

        def back(i, carry):
            b = blocks - 1 - i
            rows = pl.ds(pl.multiple_of(b * BLK, BLK), BLK)
            u, v, ca, cb, cc, o = [cols[k, rows, :] for k in range(6)]
            shade = [cols[k, rows, :] for k in (6, 7, 8)]
            dx = px - u
            sums = [0.0] * 9
            result = []
            for h in range(2):
                alpha, before = alpha_ref[h, rows, :], through_ref[h, rows, :]
                dy = py[h] - v
                weight = alpha * before
                pull = shade[0] * miss[h][0] + shade[1] * miss[h][1] + shade[2] * miss[h][2]
                run = pull * weight
                for s in (1, 2, 4, 8, 16):
                    run = run + jnp.where(row_b < BLK - s, pltpu.roll(run, BLK - s, 0), 0.0)
                after = carry[h] + jnp.where(row_b < BLK - 1, pltpu.roll(run, BLK - 1, 0), 0.0)
                result.append(carry[h] + run[0:1, :])
                slope = (before * pull - after / (1.0 - alpha)) * alpha
                tilt_x, tilt_y = slope * dx, slope * dy
                terms = [tilt_x, tilt_y, tilt_x * dx, tilt_x * dy, tilt_y * dy, slope]
                terms = terms + [weight * miss[h][k] for k in range(3)]
                sums = [a + t for a, t in zip(sums, terms)]
            m_x, m_y, m_xx, m_xy, m_yy, m_0, *g_shade = [jnp.sum(s, axis=1, keepdims=True) for s in sums]
            grads = [
                ca * m_x + cb * m_y,
                cb * m_x + cc * m_y,
                -0.5 * m_xx,
                -m_xy,
                -0.5 * m_yy,
                m_0 / o,
            ] + g_shade
            keep = cols[9, rows, :]
            for m in range(ROWS):
                value = jnp.zeros((BLK, 128), F32)
                for q in range(4):
                    if 4 * m + q < 9:
                        value = jnp.where(lane_b // 32 == q, jnp.broadcast_to(grads[4 * m + q], (BLK, 128)), value)
                lost[rows, m * 128 : (m + 1) * 128] = value * keep
            return tuple(result)

        lax.fori_loop(0, blocks, back, (zero, zero))
        tall = lax.broadcasted_iota(jnp.int32, (N_DEV, LIST), 0)
        giver = jnp.where(tall == list_row[p] // 8, 1.0, 0.0).astype(BF16)
        part = pick(giver, lost[...])
        total = part if total is None else total + part
    for m in range(ROWS):
        out[:, m, :] = total[:, m * 128 : (m + 1) * 128]


def gradient_kernel(
    cam, pos, scl, rot, opa, col, table, arrived, g_pos, g_scl, g_rot, g_opa, g_col, flat, wide, slope, view_ref, cot
):
    for k, value in enumerate(view_of(cam)):
        view_ref[k] = value
    expand((pos, scl, rot, opa, col), flat, wide)
    lane = lax.broadcasted_iota(jnp.int32, (64, 128), 1)
    even = lax.rem(lane // 16, 2) == 0
    for g in range(N_CAM):
        wanted = table[g * N_TILE : (g + 1) * N_TILE, 0, :]
        chooser = jnp.where(wanted == lax.rem(lane, 64), 1.0, 0.0).T.astype(BF16)
        for m in range(ROWS):
            both = pick(chooser, arrived[g * N_TILE : (g + 1) * N_TILE, m, :])
            value = jnp.where(even, both[0:64], both[64:128])
            for q in range(4):
                v = 4 * m + q
                if v < 9:
                    turned = turn(value, (g - q) * 32)
                    if g == 0:
                        cot[v] = turned
                    else:
                        cot[v] = jnp.where(lane // 32 == g, turned, cot[v])

    def step(chunk, carry):
        view = [view_ref[k] for k in range(15)]
        raw = [wide[chunk * 64 + k] for k in range(59)]
        rows = pl.ds(pl.multiple_of(chunk * 8, 8), 8)
        _, pull = jax.vjp(lambda values: project(values, view), raw)
        (grads,) = pull([cot[v, rows, :] for v in range(9)])
        for k in range(59):
            slope[chunk * 64 + k] = grads[k]
        for k in range(59, 64):
            slope[chunk * 64 + k] = jnp.zeros((8, 128), F32)
        return carry

    lax.fori_loop(0, 8, step, 0)
    total = jnp.zeros((512, 128), F32)
    into = lax.broadcasted_iota(jnp.int32, (256, 128), 1)
    taken = lax.broadcasted_iota(jnp.int32, (256, 128), 0)
    for i in range(0, 8, 2):
        gather = jnp.where((into // 16 == i + taken // 128) & (lax.rem(into, 16) == lax.rem(taken, 16)), 1.0, 0.0).astype(BF16)
        high, mid, low = split(jnp.concatenate([slope[:, i, :], slope[:, i + 1, :]], axis=1))
        total = total + (
            (jnp.dot(high, gather, preferred_element_type=F32) + jnp.dot(mid, gather, preferred_element_type=F32))
            + jnp.dot(low, gather, preferred_element_type=F32)
        )
    for j in range(8):
        start = j * 64
        for ref in (g_pos, g_scl, g_rot, g_opa, g_col):
            ref[:, j * 128 : (j + 1) * 128] = total[start : start + ref.shape[0], :]
            start += ref.shape[0]


VMEM = pl.BlockSpec(memory_space=pltpu.VMEM)
SMEM = pl.BlockSpec(memory_space=pltpu.SMEM)
DMA = pltpu.SemaphoreType.DMA


def shape(*dims, dtype=F32):
    return jax.ShapeDtypeStruct(dims, dtype)


def body(
    positions,
    log_scales,
    rotations,
    opacities,
    colors,
    cameras,
    targets,
    tile_ids,
    tile_counts,
    tile_lists,
    fetch_ids,
):
    params = (positions, log_scales, rotations, opacities.reshape(1, 1024), colors)
    fetched = fetch_ids.reshape(2, N_DEV, 8)
    block = fetched[:, 0, 0] // 16
    mine = jnp.repeat(block, 64).reshape(1, 1, 128)
    lists = tile_lists.reshape(2, LIST)
    spread_scratch = [
        pltpu.VMEM((64, 1024), F32),
        pltpu.VMEM((512, 8, 128), F32),
    ]
    table, returned = pl.pallas_call(
        main_kernel,
        out_shape=(shape(N_DEV, 1, 128, dtype=jnp.int32), shape(N_DEV, ROWS, 128)),
        in_specs=[SMEM] * 3 + [VMEM] * 10,
        out_specs=(VMEM, VMEM),
        scratch_shapes=spread_scratch
        + [
            pltpu.VMEM((15, 8, 128), F32),
            pltpu.VMEM((12, 64, 128), F32),
            pltpu.VMEM((N_DEV, ROWS, 128), F32),
            pltpu.VMEM((N_DEV, ROWS, 128), F32),
            pltpu.VMEM((N_DEV, ROWS, 128), F32),
            pltpu.VMEM((10, LIST, 128), F32),
            pltpu.VMEM((2, LIST, 128), F32),
            pltpu.VMEM((2, LIST, 128), F32),
            pltpu.VMEM((LIST, 3 * 128), F32),
        ]
        + [DMA] * 11,
        compiler_params=pltpu.CompilerParams(collective_id=0, has_side_effects=True),
    )(
        tile_ids.reshape(2),
        tile_counts.reshape(2),
        cameras,
        *params,
        mine,
        fetched,
        lists.reshape(2, LIST, 1),
        lists.reshape(2, 1, LIST),
        targets.reshape(2, 3, PIX),
    )

    g_pos, g_scl, g_rot, g_opa, g_col = pl.pallas_call(
        gradient_kernel,
        out_shape=tuple(shape(n, 1024) for n in (3, 3, 4, 1, 48)),
        in_specs=[SMEM] + [VMEM] * 7,
        out_specs=(VMEM,) * 5,
        scratch_shapes=spread_scratch
        + [
            pltpu.VMEM((512, 8, 128), F32),
            pltpu.VMEM((15, 8, 128), F32),
            pltpu.VMEM((9, 64, 128), F32),
        ],
    )(cameras, *params, table, returned)
    return g_pos, g_scl, g_rot, g_opa.reshape(1024), g_col


def solution(mesh):
    return jax.shard_map(
        body,
        mesh=mesh,
        in_specs=(
            P(None, ("cam", "tile")),
            P(None, ("cam", "tile")),
            P(None, ("cam", "tile")),
            P(("cam", "tile")),
            P(None, ("cam", "tile")),
            P(),
            P(None, "cam", "tile", None, None),
            P(None, "cam", "tile"),
            P(None, "cam", "tile"),
            P(None, "cam", "tile", None),
            P(None, "cam", "tile", None, None, None),
        ),
        out_specs=(
            P(None, ("cam", "tile")),
            P(None, ("cam", "tile")),
            P(None, ("cam", "tile")),
            P(("cam", "tile")),
            P(None, ("cam", "tile")),
        ),
        check_vma=False,
    )
```

```python
import jax
import jax.numpy as jnp
from jax import lax
from jax.experimental import pallas as pl
from jax.experimental.pallas import tpu as pltpu
from jax.sharding import PartitionSpec as P

N_CAM, N_TILE, N_DEV = 4, 64, 256
LIST, PIX, BLK = 256, 256, 32
MESH = pl.DeviceIdType.MESH
F32, BF16 = jnp.float32, jnp.bfloat16

FOCAL = 4096.0
SH_ZERO = 0.28209479177387814
SH_ONE = 0.4886025119029199
SH_TWO = [
    1.0925484305920792,
    -1.0925484305920792,
    0.31539156525252005,
    -1.0925484305920792,
    0.5462742152960396,
]
SH_THREE = [
    -0.5900435899266435,
    2.890611442640554,
    -0.4570457994644658,
    0.3731763325901154,
    -0.4570457994644658,
    1.445305721320277,
    -0.5900435899266435,
]


def matmul3(left, right):
    return [
        [
            left[i][0] * right[0][j] + left[i][1] * right[1][j] + left[i][2] * right[2][j]
            for j in range(3)
        ]
        for i in range(3)
    ]


def view_of(cam_ref, view):
    values = []
    for k in range(6):
        value = jnp.zeros((8, 128), F32)
        for c in range(N_CAM):
            for p in range(2):
                value = jnp.where(view == c * 2 + p, cam_ref[p, c, k], value)
        values.append(value)
    cos_a, sin_a = jnp.cos(values[0]), jnp.sin(values[0])
    cos_b, sin_b = jnp.cos(values[1]), jnp.sin(values[1])
    cos_c, sin_c = jnp.cos(values[2]), jnp.sin(values[2])
    rotate = [
        [cos_c * cos_b, cos_c * sin_b * sin_a - sin_c * cos_a, cos_c * sin_b * cos_a + sin_c * sin_a],
        [sin_c * cos_b, sin_c * sin_b * sin_a + cos_c * cos_a, sin_c * sin_b * cos_a - cos_c * sin_a],
        [-sin_b, cos_b * sin_a, cos_b * cos_a],
    ]
    offset = [values[3], values[4], 6.0 + values[5]]
    anchor = [
        -(rotate[0][j] * offset[0] + rotate[1][j] * offset[1] + rotate[2][j] * offset[2])
        for j in range(3)
    ]
    return [rotate[i][j] for i in range(3) for j in range(3)] + offset + anchor


def covariance_of(raw):
    quat_norm = jnp.sqrt(raw[3] * raw[3] + raw[4] * raw[4] + raw[5] * raw[5] + raw[6] * raw[6])
    per_norm = 1.0 / quat_norm
    qw, qx, qy, qz = (raw[3] * per_norm, raw[4] * per_norm, raw[5] * per_norm, raw[6] * per_norm)
    spin = [
        [1.0 - 2.0 * (qy * qy + qz * qz), 2.0 * (qx * qy - qw * qz), 2.0 * (qx * qz + qw * qy)],
        [2.0 * (qx * qy + qw * qz), 1.0 - 2.0 * (qx * qx + qz * qz), 2.0 * (qy * qz - qw * qx)],
        [2.0 * (qx * qz - qw * qy), 2.0 * (qy * qz + qw * qx), 1.0 - 2.0 * (qx * qx + qy * qy)],
    ]
    squares = [jnp.exp(2.0 * raw[k]) for k in range(3)]
    return [
        spin[i][0] * spin[j][0] * squares[0]
        + spin[i][1] * spin[j][1] * squares[1]
        + spin[i][2] * spin[j][2] * squares[2]
        for i, j in ((0, 0), (0, 1), (0, 2), (1, 1), (1, 2), (2, 2))
    ]


def screen_of(point, cov, colors, view):
    rotate = [view[0:3], view[3:6], view[6:9]]
    offset, anchor = view[9:12], view[12:15]
    viewed = [
        rotate[i][0] * point[0] + rotate[i][1] * point[1] + rotate[i][2] * point[2] + offset[i]
        for i in range(3)
    ]
    toward = [point[j] - anchor[j] for j in range(3)]
    length = jnp.sqrt(toward[0] * toward[0] + toward[1] * toward[1] + toward[2] * toward[2])
    per_length = 1.0 / length
    ux, uy, uz = (toward[0] * per_length, toward[1] * per_length, toward[2] * per_length)
    world = [[cov[0], cov[1], cov[2]], [cov[1], cov[3], cov[4]], [cov[2], cov[4], cov[5]]]
    half_way = matmul3(rotate, world)

    def seen(a, b):
        return (
            half_way[a][0] * rotate[b][0] + half_way[a][1] * rotate[b][1] + half_way[a][2] * rotate[b][2]
        )

    c00, c01, c02 = seen(0, 0), seen(0, 1), seen(0, 2)
    c11, c12, c22 = seen(1, 1), seen(1, 2), seen(2, 2)
    inverse = 1.0 / viewed[2]
    j_main = FOCAL * inverse
    j_side_x = -j_main * viewed[0] * inverse
    j_side_y = -j_main * viewed[1] * inverse
    s_xx = j_main * j_main * c00 + 2.0 * j_main * j_side_x * c02 + j_side_x * j_side_x * c22 + 0.3
    s_xy = (
        j_main * j_main * c01
        + j_main * j_side_y * c02
        + j_side_x * j_main * c12
        + j_side_x * j_side_y * c22
    )
    s_yy = j_main * j_main * c11 + 2.0 * j_main * j_side_y * c12 + j_side_y * j_side_y * c22 + 0.3
    per_det = 1.0 / (s_xx * s_yy - s_xy * s_xy)
    xx, yy, zz = (ux * ux, uy * uy, uz * uz)
    basis = [
        None,
        -SH_ONE * uy,
        SH_ONE * uz,
        -SH_ONE * ux,
        SH_TWO[0] * ux * uy,
        SH_TWO[1] * uy * uz,
        SH_TWO[2] * (2.0 * zz - xx - yy),
        SH_TWO[3] * ux * uz,
        SH_TWO[4] * (xx - yy),
        SH_THREE[0] * uy * (3.0 * xx - yy),
        SH_THREE[1] * ux * uy * uz,
        SH_THREE[2] * uy * (4.0 * zz - xx - yy),
        SH_THREE[3] * uz * (2.0 * zz - 3.0 * xx - 3.0 * yy),
        SH_THREE[4] * ux * (4.0 * zz - xx - yy),
        SH_THREE[5] * uz * (xx - yy),
        SH_THREE[6] * ux * (xx - 3.0 * yy),
    ]
    channels = []
    for channel in range(3):
        total = 0.5 + SH_ZERO * colors[channel]
        for k in range(1, 16):
            total = total + basis[k] * colors[3 * k + channel]
        channels.append(total)
    return [
        j_main * viewed[0] + 2048.0,
        j_main * viewed[1] + 1024.0,
        s_yy * per_det,
        -s_xy * per_det,
        s_xx * per_det,
    ] + channels


def sigmoid(value):
    return 1.0 / (1.0 + jnp.exp(-value))


def split(value):
    high = value.astype(BF16)
    rest = value - high.astype(F32)
    mid = rest.astype(BF16)
    low = (rest - mid.astype(F32)).astype(BF16)
    return high, mid, low


def pick(chooser, value):
    high, mid, low = split(value)
    return (
        jnp.dot(chooser, high, preferred_element_type=F32)
        + jnp.dot(chooser, mid, preferred_element_type=F32)
    ) + jnp.dot(chooser, low, preferred_element_type=F32)


def pick_two(chooser, value):
    high = value.astype(BF16)
    mid = (value - high.astype(F32)).astype(BF16)
    return jnp.dot(chooser, high, preferred_element_type=F32) + jnp.dot(chooser, mid, preferred_element_type=F32)


def turn(value, lanes):
    lanes = lanes % 128
    return value if lanes == 0 else pltpu.roll(value, lanes, 1)


def spread_of(first):
    lane = lax.broadcasted_iota(jnp.int32, (128, 256), 1)
    row = lax.broadcasted_iota(jnp.int32, (128, 256), 0)
    return jnp.where(row == (first + lane // 128) * 16 + lax.rem(lane, 16), 1.0, 0.0).astype(BF16)


def expand(refs, flat, wide):
    flat[56:64, :] = jnp.zeros((8, 1024), F32)
    start = 0
    for ref in refs:
        flat[start : start + ref.shape[0], :] = ref[...]
        start += ref.shape[0]
    parts = split(jnp.concatenate([flat[:, j * 128 : (j + 1) * 128] for j in range(8)], axis=0))
    for i in range(0, 8, 2):
        spread = spread_of(i)
        value = (
            jnp.dot(parts[0], spread, preferred_element_type=F32)
            + jnp.dot(parts[1], spread, preferred_element_type=F32)
        ) + jnp.dot(parts[2], spread, preferred_element_type=F32)
        wide[:, i, :] = value[:, 0:128]
        wide[:, i + 1, :] = value[:, 128:256]


def project_chunk(chunk, wide, view_ref, out):
    view = [view_ref[k] for k in range(15)]
    raw = [wide[chunk * 64 + k] for k in range(59)]
    record = screen_of(raw[0:3], covariance_of(raw[3:10]), raw[11:], view)
    slot = lax.broadcasted_iota(jnp.int32, (8, 128), 1) // 16
    rows = pl.ds(pl.multiple_of(chunk * 8, 8), 8)
    for v in range(8):
        value = turn(record[0], -v * 16)
        for k in range(1, 8):
            value = jnp.where(slot == k, turn(record[k], (k - v) * 16), value)
        out[v, rows, :] = value
    out[8, rows, :] = sigmoid(raw[10])


def place():
    return lax.axis_index("cam"), lax.axis_index("tile")


def across(c, t, i):
    index = lax.rem(c * 4 + t // 16 + i, 16)
    return (index // 4, lax.rem(index, 4) * 16 + lax.rem(t, 16))


def along(c, t, i):
    return (c, (t // 16) * 16 + lax.rem(lax.rem(t, 16) + i, 16))


def greet(c, t):
    barrier = pltpu.get_barrier_semaphore()

    def hail(i, carry):
        pl.semaphore_signal(barrier, inc=1, device_id=along(c, t, i), device_id_type=MESH)
        pl.semaphore_signal(barrier, inc=1, device_id=across(c, t, i), device_id_type=MESH)
        return carry

    lax.fori_loop(1, 16, hail, 0)
    return barrier


def send_rows(src, dst, c, t, send, recv):
    me = c * N_TILE + t

    def one(i, carry):
        to = lax.rem(me + i, N_DEV)
        pltpu.make_async_remote_copy(
            src_ref=src.at[to],
            dst_ref=dst.at[me],
            send_sem=send,
            recv_sem=recv,
            device_id=(to // N_TILE, lax.rem(to, N_TILE)),
            device_id_type=MESH,
        ).start()
        return carry

    lax.fori_loop(1, N_DEV, one, 0, unroll=5)


def wait_rows(src, dst, send, recv):
    most = pl.ds(0, N_DEV - 1)
    pltpu.make_async_copy(src.at[most], src.at[most], send).wait()
    pltpu.make_async_copy(dst.at[most], dst.at[most], recv).wait()


def chooser_of(table, g):
    wanted = table[g * N_TILE : (g + 1) * N_TILE, 0, :]
    lane = lax.broadcasted_iota(jnp.int32, (64, 128), 1)
    return jnp.where(wanted == lax.rem(lane, 64), 1.0, 0.0)


def main_kernel(
    place_ref,
    count_ref,
    cam,
    pos,
    scl,
    rot,
    opa,
    col,
    fetch,
    lists,
    target,
    table,
    back_0,
    back_1,
    mine,
    flat,
    wide,
    view_ref,
    records,
    out_0,
    out_1,
    data_0,
    data_1,
    grad_0,
    grad_1,
    chosen,
    givers,
    spots,
    cols,
    alpha_ref,
    through_ref,
    lost,
    send_a,
    recv_a,
    send_b,
    recv_b,
    send_c,
    recv_c,
    send_d,
    recv_d,
    send_e,
    recv_e,
    send_f,
    recv_f,
    own_a,
    own_c,
    own_d,
    own_e,
    own_f,
):
    c, t = place()
    me = c * N_TILE + t
    barrier = greet(c, t)
    block = [fetch[p, 0, 0:1, 0:1] // 16 for p in range(2)]
    half = lax.broadcasted_iota(jnp.int32, (1, 128), 1) < 64
    mine[0, :, :] = jnp.where(half, jnp.broadcast_to(block[0], (1, 128)), jnp.broadcast_to(block[1], (1, 128)))
    for k, value in enumerate(view_of(cam, lax.broadcasted_iota(jnp.int32, (8, 128), 1) // 16)):
        view_ref[k] = value
    expand((pos, scl, rot, opa, col), flat, wide)

    def step(chunk, carry):
        project_chunk(chunk, wide, view_ref, records)
        return carry

    local = pltpu.make_async_copy(mine.at[0], table.at[me], own_a)
    local.start()
    pl.semaphore_wait(barrier, 30)

    def first(i, carry):
        pltpu.make_async_remote_copy(
            src_ref=mine.at[0],
            dst_ref=table.at[me],
            send_sem=send_a,
            recv_sem=recv_a,
            device_id=along(c, t, i),
            device_id_type=MESH,
        ).start()
        return carry

    lax.fori_loop(1, 16, first, 0)
    lax.fori_loop(0, 8, step, 0)
    local.wait()
    some = pl.ds(0, 15)
    pltpu.make_async_copy(table.at[some], table.at[some], send_a).wait()
    pltpu.make_async_copy(table.at[some], table.at[some], recv_a).wait()
    line = pl.ds(c * N_TILE + (t // 16) * 16, 16)

    def second(i, carry):
        pltpu.make_async_remote_copy(
            src_ref=table.at[line],
            dst_ref=table.at[line],
            send_sem=send_b,
            recv_sem=recv_b,
            device_id=across(c, t, i),
            device_id_type=MESH,
        ).start()
        return carry

    lax.fori_loop(1, 16, second, 0)
    for p in range(2):
        prepare(p, fetch, lists, chosen, givers, spots)
    most = pl.ds(0, 240)
    pltpu.make_async_copy(table.at[most], table.at[most], send_b).wait()
    pltpu.make_async_copy(table.at[most], table.at[most], recv_b).wait()

    lane = lax.broadcasted_iota(jnp.int32, (64, 128), 1)
    opacity = records[8]
    opacity = [jnp.where(lane // 16 == p, opacity, 0.0) for p in range(2)]
    none = jnp.zeros((64, 128), F32)
    for g in range(N_CAM):
        chooser = chooser_of(table, g).astype(BF16)
        upper = jnp.concatenate([records[2 * g], opacity[0], none], axis=1)
        lower = jnp.concatenate([none, opacity[1], records[2 * g + 1]], axis=1)
        value = pick(chooser, jnp.concatenate([upper, lower], axis=0))
        here = pl.ds(g * N_TILE, N_TILE)
        out_0[here, 0, :] = value[:, 0:128]
        out_0[here, 1, :] = value[:, 128:256]
        out_1[here, 0, :] = value[:, 256:384]
    local_0 = pltpu.make_async_copy(out_0.at[me], data_0.at[me], own_c)
    local_0.start()
    send_rows(out_0, data_0, c, t, send_c, recv_c)
    local_1 = pltpu.make_async_copy(out_1.at[me], data_1.at[me], own_d)
    local_1.start()
    send_rows(out_1, data_1, c, t, send_d, recv_d)
    local_0.wait()
    wait_rows(out_0, data_0, send_c, recv_c)
    opacity = data_0[:, 1, :]
    shared = (place_ref, count_ref, chosen, givers, spots, target, cols, alpha_ref, through_ref, lost)
    given_0, given_o = render(0, data_0[:, 0, :], opacity, *shared)
    grad_0[:, 0, :] = given_0
    local_0 = pltpu.make_async_copy(grad_0.at[me], back_0.at[me], own_e)
    local_0.start()
    send_rows(grad_0, back_0, c, t, send_e, recv_e)
    local_1.wait()
    wait_rows(out_1, data_1, send_d, recv_d)
    grad_1[:, 1, :] = given_o
    given_1, given_o = render(1, data_1[:, 0, :], opacity, *shared)
    grad_1[:, 0, :] = given_1
    grad_1[:, 1, :] = grad_1[:, 1, :] + given_o
    local_1 = pltpu.make_async_copy(grad_1.at[me], back_1.at[me], own_f)
    local_1.start()
    send_rows(grad_1, back_1, c, t, send_f, recv_f)
    local_0.wait()
    wait_rows(grad_0, back_0, send_e, recv_e)
    local_1.wait()
    wait_rows(grad_1, back_1, send_f, recv_f)


def prepare(p, fetch, lists, chosen, givers, spots):
    wide = lax.broadcasted_iota(jnp.int32, (LIST, N_DEV), 1)
    tall = lax.broadcasted_iota(jnp.int32, (LIST, N_DEV), 0)
    listed = jnp.broadcast_to(lists[p], (LIST, N_DEV)).astype(F32)
    slot = jnp.sum(jnp.where(wide == lax.rem(tall, 8) * 32 + tall // 8, listed, 0.0), axis=1, keepdims=True)
    slot = slot.astype(jnp.int32)
    chooser = jnp.where(wide == slot // 8, 1.0, 0.0)
    givers[p] = chooser.T.astype(BF16)
    chooser = chooser.astype(BF16)
    chosen[p] = chooser
    within = jnp.concatenate([lax.rem(fetch[p, g], 16).astype(F32) for g in range(N_CAM)], axis=1).astype(BF16)
    near = lax.dot_general(chooser, within, (((1,), (1,)), ((), ())), preferred_element_type=F32)
    eight = lax.broadcasted_iota(jnp.int32, near.shape, 1)
    column = jnp.sum(jnp.where(eight == lax.rem(slot, 8), near, 0.0), axis=1, keepdims=True)
    spots[p] = jnp.broadcast_to(column, (LIST, 128)).astype(jnp.int32)


def before_of(run):
    row = lax.broadcasted_iota(jnp.int32, (8, 128), 0)
    for s in (1, 2, 4):
        run = run * jnp.where(row >= s, pltpu.roll(run, s, 0), 1.0)
    return jnp.where(row >= 1, pltpu.roll(run, 1, 0), 1.0)


def after_of(run):
    row = lax.broadcasted_iota(jnp.int32, (8, 128), 0)
    for s in (1, 2, 4):
        run = run + jnp.where(row < 8 - s, pltpu.roll(run, 8 - s, 0), 0.0)
    return jnp.where(row < 7, pltpu.roll(run, 7, 0), 0.0)


def render(p, data, opacity, place_ref, count_ref, chosen, givers, spots, target, cols, alpha_ref, through_ref, lost):
    lane_b = lax.broadcasted_iota(jnp.int32, (BLK, 128), 1)
    row_b = lax.broadcasted_iota(jnp.int32, (BLK, 128), 0)
    lane_1 = lax.broadcasted_iota(jnp.int32, (1, 128), 1)
    blocks, parts = LIST // BLK, BLK // 8
    picked = pick(chosen[p], jnp.concatenate([data, opacity], axis=1))
    spot = spots[p]
    for k in range(9):
        source, first = (picked[:, 128:256], p * 16) if k == 8 else (picked[:, 0:128], k * 16)
        cols[k] = jnp.take_along_axis(source, spot + first, axis=1)

    tile = place_ref[p]
    count = count_ref[p]
    left = (lax.rem(tile, 256) * 16).astype(F32) + 0.5
    top = ((tile // 256) * 16).astype(F32) + 0.5
    px = left + lax.rem(lane_1, 16).astype(F32)
    py = [top + ((lane_1 + h * 128) // 16).astype(F32) for h in range(2)]

    def ahead(b, carry):
        rows = pl.ds(pl.multiple_of(b * BLK, BLK), BLK)
        u, v, ca, cb, cc = [cols[k, rows, :] for k in range(5)]
        shade = [cols[k, rows, :] for k in (5, 6, 7)]
        o = cols[8, rows, :]
        live = lax.rem(row_b, 8) * 32 + row_b // 8 + b * parts < count
        dx = px - u
        dxx = ca * dx * dx
        result = []
        for h in range(2):
            run, shown = carry[h][0], list(carry[h][1:])
            dy = py[h] - v
            quad = dxx + 2.0 * cb * dx * dy + cc * dy * dy
            alpha = jnp.where(live, o * jnp.exp(-0.5 * quad), 0.0)
            alpha_ref[h, rows, :] = alpha
            keep = 1.0 - alpha
            before = []
            for n in range(parts):
                before.append(run)
                run = run * keep[8 * n : 8 * n + 8]
            before = jnp.concatenate(before, axis=0)
            through_ref[h, rows, :] = before
            weight = alpha * before
            for k in range(3):
                value = shade[k] * weight
                for n in range(parts):
                    shown[k] = shown[k] + value[8 * n : 8 * n + 8]
            result.append((run, *shown))
        return tuple(result)

    one, zero = jnp.ones((8, 128), F32), jnp.zeros((8, 128), F32)
    state = lax.fori_loop(0, blocks, ahead, ((one, zero, zero, zero),) * 2)
    ahead_of, miss, behind = [], [], []
    for h in range(2):
        prefix = before_of(state[h][0])
        parts_of = [prefix * state[h][1 + k] for k in range(3)]
        gap = [
            jnp.sum(parts_of[k], axis=0, keepdims=True) - target[p, k, :, h * 128 : (h + 1) * 128]
            for k in range(3)
        ]
        ahead_of.append(jnp.concatenate([prefix] * parts, axis=0))
        miss.append(gap)
        behind.append(after_of(gap[0] * parts_of[0] + gap[1] * parts_of[1] + gap[2] * parts_of[2]))

    def back(i, carry):
        b = blocks - 1 - i
        rows = pl.ds(pl.multiple_of(b * BLK, BLK), BLK)
        u, v, ca, cb, cc = [cols[k, rows, :] for k in range(5)]
        shade = [cols[k, rows, :] for k in (5, 6, 7)]
        o = cols[8, rows, :]
        dx = px - u
        sums = [0.0] * 9
        result = []
        for h in range(2):
            alpha = alpha_ref[h, rows, :]
            before = through_ref[h, rows, :] * ahead_of[h]
            dy = py[h] - v
            weight = alpha * before
            pull = shade[0] * miss[h][0] + shade[1] * miss[h][1] + shade[2] * miss[h][2]
            value = pull * weight
            run = carry[h]
            after = []
            for n in reversed(range(parts)):
                after.insert(0, run)
                run = run + value[8 * n : 8 * n + 8]
            result.append(run)
            after = jnp.concatenate(after, axis=0)
            slope = (before * pull - after / (1.0 - alpha)) * alpha
            tilt_x, tilt_y = slope * dx, slope * dy
            terms = [tilt_x, tilt_y, tilt_x * dx, tilt_x * dy, tilt_y * dy, slope]
            terms = terms + [weight * miss[h][k] for k in range(3)]
            sums = [x + y for x, y in zip(sums, terms)]
        m_x, m_y, m_xx, m_xy, m_yy, m_0, *g_shade = [jnp.sum(x, axis=1, keepdims=True) for x in sums]
        grads = [ca * m_x + cb * m_y, cb * m_x + cc * m_y, -0.5 * m_xx, -m_xy, -0.5 * m_yy] + g_shade
        spot_b = spots[p, rows, :]
        value = jnp.zeros((BLK, 128), F32)
        for k in range(8):
            value = jnp.where(lane_b == spot_b + k * 16, jnp.broadcast_to(grads[k], (BLK, 128)), value)
        lost[rows, 0:128] = value
        lost[rows, 128:256] = jnp.where(lane_b == spot_b + p * 16, m_0 / o, 0.0)
        return tuple(result)

    lax.fori_loop(0, blocks, back, tuple(behind))
    given = pick_two(givers[p], lost[...])
    return given[:, 0:128], given[:, 128:256]


def gradient_kernel(
    cam, pos, scl, rot, opa, col, table, back_0, back_1, g_pos, g_scl, g_rot, g_opa, g_col, raw, view_ref, cot, total
):
    row = lax.broadcasted_iota(jnp.int32, (8, 128), 0)
    lane = lax.broadcasted_iota(jnp.int32, (8, 128), 1)
    for k, value in enumerate(view_of(cam, row)):
        view_ref[k] = value
    start = 0
    for ref in (pos, scl, rot, opa, col):
        for j in range(8):
            raw[start : start + ref.shape[0], j, :] = ref[:, j * 128 : (j + 1) * 128]
        start += ref.shape[0]

    def fold(value, first):
        out = jnp.zeros((8, 128), F32)
        for j in range(8):
            part = jnp.take_along_axis(value[8 * j : 8 * j + 8], first + lax.rem(lane, 16), axis=1)
            part = jnp.take_along_axis(part, lane // 16, axis=0)
            out = jnp.where(row == j, part, out)
        return out

    opacity = jnp.zeros((8, 128), F32)
    for g in range(N_CAM):
        chooser = chooser_of(table, g).T.astype(BF16)
        here = pl.ds(g * N_TILE, N_TILE)
        sent = jnp.concatenate([back_0[here, 0, :], back_1[here, 1, :], back_1[here, 0, :]], axis=1)
        value = pick_two(chooser, sent)
        for p in range(2):
            part = value[p * 64 : p * 64 + 64, p * 256 : p * 256 + 128]
            for v in range(8):
                cot[2 * g + p, v] = fold(part, v * 16)
            opacity = opacity + fold(value[p * 64 : p * 64 + 64, 128:256], p * 16)
    for k in range(57):
        total[k] = jnp.zeros((8, 128), F32)
    shape_raw = [raw[k] for k in range(3, 10)]
    for k, value in enumerate(covariance_of(shape_raw)):
        cot[8, k] = value

    def step(v, carry):
        view = [view_ref[k, pl.ds(v, 1), :] for k in range(15)]
        point = [raw[k] for k in range(3)]
        cov = [cot[8, k] for k in range(6)]
        colors = [raw[11 + k] for k in range(48)]
        _, pull = jax.vjp(lambda a, b, d: screen_of(a, b, d, view), point, cov, colors)
        grads = pull([cot[v, k] for k in range(8)])
        for k, value in enumerate(grads[0] + grads[1] + grads[2]):
            total[k] = total[k] + value
        return carry

    lax.fori_loop(0, 8, step, 0)
    _, pull = jax.vjp(covariance_of, [raw[k] for k in range(3, 10)])
    (shape_grads,) = pull([total[3 + k] for k in range(6)])
    for k in range(7):
        total[57 + k] = shape_grads[k]
    o = sigmoid(raw[10])
    total[3] = opacity * o * (1.0 - o)
    for j in range(8):
        here = pl.ds(j * 128, 128)
        g_pos[:, here] = total[0:3, j, :]
        g_scl[:, here] = total[57:60, j, :]
        g_rot[:, here] = total[60:64, j, :]
        g_opa[:, here] = total[3:4, j, :]
        g_col[:, here] = total[9:57, j, :]


VMEM = pl.BlockSpec(memory_space=pltpu.VMEM)
SMEM = pl.BlockSpec(memory_space=pltpu.SMEM)
DMA = pltpu.SemaphoreType.DMA


def shape(*dims, dtype=F32):
    return jax.ShapeDtypeStruct(dims, dtype)


def body(
    positions,
    log_scales,
    rotations,
    opacities,
    colors,
    cameras,
    targets,
    tile_ids,
    tile_counts,
    tile_lists,
    fetch_ids,
):
    params = (positions, log_scales, rotations, opacities.reshape(1, 1024), colors)
    single, double = pltpu.VMEM((N_DEV, 1, 128), F32), pltpu.VMEM((N_DEV, 2, 128), F32)
    table, back_0, back_1 = pl.pallas_call(
        main_kernel,
        out_shape=(shape(N_DEV, 1, 128, dtype=jnp.int32), shape(N_DEV, 1, 128), shape(N_DEV, 2, 128)),
        in_specs=[SMEM] * 3 + [VMEM] * 8,
        out_specs=(VMEM,) * 3,
        scratch_shapes=[
            pltpu.VMEM((1, 1, 128), jnp.int32),
            pltpu.VMEM((64, 1024), F32),
            pltpu.VMEM((512, 8, 128), F32),
            pltpu.VMEM((15, 8, 128), F32),
            pltpu.VMEM((9, 64, 128), F32),
            double,
            single,
            double,
            single,
            single,
            double,
            pltpu.VMEM((2, LIST, N_DEV), BF16),
            pltpu.VMEM((2, N_DEV, LIST), BF16),
            pltpu.VMEM((2, LIST, 128), jnp.int32),
            pltpu.VMEM((9, LIST, 128), F32),
            pltpu.VMEM((2, LIST, 128), F32),
            pltpu.VMEM((2, LIST, 128), F32),
            pltpu.VMEM((LIST, 2 * 128), F32),
        ]
        + [DMA] * 17,
        compiler_params=pltpu.CompilerParams(collective_id=0, has_side_effects=True),
    )(
        tile_ids.reshape(2),
        tile_counts.reshape(2),
        cameras,
        *params,
        fetch_ids.reshape(2, N_CAM, N_TILE, 8).transpose(0, 1, 3, 2),
        tile_lists.reshape(2, 1, LIST),
        targets.reshape(2, 3, 1, PIX),
    )

    g_pos, g_scl, g_rot, g_opa, g_col = pl.pallas_call(
        gradient_kernel,
        out_shape=tuple(shape(n, 1024) for n in (3, 3, 4, 1, 48)),
        in_specs=[SMEM] + [VMEM] * 8,
        out_specs=(VMEM,) * 5,
        scratch_shapes=[
            pltpu.VMEM((59, 8, 128), F32),
            pltpu.VMEM((15, 8, 128), F32),
            pltpu.VMEM((9, 8, 8, 128), F32),
            pltpu.VMEM((64, 8, 128), F32),
        ],
    )(cameras, *params, table, back_0, back_1)
    return g_pos, g_scl, g_rot, g_opa.reshape(1024), g_col


def solution(mesh):
    return jax.shard_map(
        body,
        mesh=mesh,
        in_specs=(
            P(None, ("cam", "tile")),
            P(None, ("cam", "tile")),
            P(None, ("cam", "tile")),
            P(("cam", "tile")),
            P(None, ("cam", "tile")),
            P(),
            P(None, "cam", "tile", None, None),
            P(None, "cam", "tile"),
            P(None, "cam", "tile"),
            P(None, "cam", "tile", None),
            P(None, "cam", "tile", None, None, None),
        ),
        out_specs=(
            P(None, ("cam", "tile")),
            P(None, ("cam", "tile")),
            P(None, ("cam", "tile")),
            P(("cam", "tile")),
            P(None, ("cam", "tile")),
        ),
        check_vma=False,
    )
```

```python
import jax
import jax.numpy as jnp
from jax import lax
from jax.experimental import pallas as pl
from jax.experimental.pallas import tpu as pltpu
from jax.sharding import PartitionSpec as P

N_CAM, N_TILE, N_DEV = 4, 64, 256
LIST, PIX, BLK = 256, 256, 32
MESH = pl.DeviceIdType.MESH
F32, BF16 = jnp.float32, jnp.bfloat16

FOCAL = 4096.0
SH_ZERO = 0.28209479177387814
SH_ONE = 0.4886025119029199
SH_TWO = [
    1.0925484305920792,
    -1.0925484305920792,
    0.31539156525252005,
    -1.0925484305920792,
    0.5462742152960396,
]
SH_THREE = [
    -0.5900435899266435,
    2.890611442640554,
    -0.4570457994644658,
    0.3731763325901154,
    -0.4570457994644658,
    1.445305721320277,
    -0.5900435899266435,
]


def matmul3(left, right):
    return [
        [
            left[i][0] * right[0][j] + left[i][1] * right[1][j] + left[i][2] * right[2][j]
            for j in range(3)
        ]
        for i in range(3)
    ]


def view_of(cam_ref, view):
    values = []
    for k in range(6):
        value = jnp.zeros((8, 128), F32)
        for c in range(N_CAM):
            for p in range(2):
                value = jnp.where(view == c * 2 + p, cam_ref[p, c, k], value)
        values.append(value)
    cos_a, sin_a = jnp.cos(values[0]), jnp.sin(values[0])
    cos_b, sin_b = jnp.cos(values[1]), jnp.sin(values[1])
    cos_c, sin_c = jnp.cos(values[2]), jnp.sin(values[2])
    rotate = [
        [cos_c * cos_b, cos_c * sin_b * sin_a - sin_c * cos_a, cos_c * sin_b * cos_a + sin_c * sin_a],
        [sin_c * cos_b, sin_c * sin_b * sin_a + cos_c * cos_a, sin_c * sin_b * cos_a - cos_c * sin_a],
        [-sin_b, cos_b * sin_a, cos_b * cos_a],
    ]
    offset = [values[3], values[4], 6.0 + values[5]]
    anchor = [
        -(rotate[0][j] * offset[0] + rotate[1][j] * offset[1] + rotate[2][j] * offset[2])
        for j in range(3)
    ]
    return [rotate[i][j] for i in range(3) for j in range(3)] + offset + anchor


def covariance_of(raw):
    quat_norm = jnp.sqrt(raw[3] * raw[3] + raw[4] * raw[4] + raw[5] * raw[5] + raw[6] * raw[6])
    per_norm = 1.0 / quat_norm
    qw, qx, qy, qz = (raw[3] * per_norm, raw[4] * per_norm, raw[5] * per_norm, raw[6] * per_norm)
    spin = [
        [1.0 - 2.0 * (qy * qy + qz * qz), 2.0 * (qx * qy - qw * qz), 2.0 * (qx * qz + qw * qy)],
        [2.0 * (qx * qy + qw * qz), 1.0 - 2.0 * (qx * qx + qz * qz), 2.0 * (qy * qz - qw * qx)],
        [2.0 * (qx * qz - qw * qy), 2.0 * (qy * qz + qw * qx), 1.0 - 2.0 * (qx * qx + qy * qy)],
    ]
    squares = [jnp.exp(2.0 * raw[k]) for k in range(3)]
    return [
        spin[i][0] * spin[j][0] * squares[0]
        + spin[i][1] * spin[j][1] * squares[1]
        + spin[i][2] * spin[j][2] * squares[2]
        for i, j in ((0, 0), (0, 1), (0, 2), (1, 1), (1, 2), (2, 2))
    ]


def screen_of(point, cov, colors, view):
    rotate = [view[0:3], view[3:6], view[6:9]]
    offset, anchor = view[9:12], view[12:15]
    viewed = [
        rotate[i][0] * point[0] + rotate[i][1] * point[1] + rotate[i][2] * point[2] + offset[i]
        for i in range(3)
    ]
    toward = [point[j] - anchor[j] for j in range(3)]
    length = jnp.sqrt(toward[0] * toward[0] + toward[1] * toward[1] + toward[2] * toward[2])
    per_length = 1.0 / length
    ux, uy, uz = (toward[0] * per_length, toward[1] * per_length, toward[2] * per_length)
    world = [[cov[0], cov[1], cov[2]], [cov[1], cov[3], cov[4]], [cov[2], cov[4], cov[5]]]
    half_way = matmul3(rotate, world)

    def seen(a, b):
        return (
            half_way[a][0] * rotate[b][0] + half_way[a][1] * rotate[b][1] + half_way[a][2] * rotate[b][2]
        )

    c00, c01, c02 = seen(0, 0), seen(0, 1), seen(0, 2)
    c11, c12, c22 = seen(1, 1), seen(1, 2), seen(2, 2)
    inverse = 1.0 / viewed[2]
    j_main = FOCAL * inverse
    j_side_x = -j_main * viewed[0] * inverse
    j_side_y = -j_main * viewed[1] * inverse
    s_xx = j_main * j_main * c00 + 2.0 * j_main * j_side_x * c02 + j_side_x * j_side_x * c22 + 0.3
    s_xy = (
        j_main * j_main * c01
        + j_main * j_side_y * c02
        + j_side_x * j_main * c12
        + j_side_x * j_side_y * c22
    )
    s_yy = j_main * j_main * c11 + 2.0 * j_main * j_side_y * c12 + j_side_y * j_side_y * c22 + 0.3
    per_det = 1.0 / (s_xx * s_yy - s_xy * s_xy)
    xx, yy, zz = (ux * ux, uy * uy, uz * uz)
    basis = [
        None,
        -SH_ONE * uy,
        SH_ONE * uz,
        -SH_ONE * ux,
        SH_TWO[0] * ux * uy,
        SH_TWO[1] * uy * uz,
        SH_TWO[2] * (2.0 * zz - xx - yy),
        SH_TWO[3] * ux * uz,
        SH_TWO[4] * (xx - yy),
        SH_THREE[0] * uy * (3.0 * xx - yy),
        SH_THREE[1] * ux * uy * uz,
        SH_THREE[2] * uy * (4.0 * zz - xx - yy),
        SH_THREE[3] * uz * (2.0 * zz - 3.0 * xx - 3.0 * yy),
        SH_THREE[4] * ux * (4.0 * zz - xx - yy),
        SH_THREE[5] * uz * (xx - yy),
        SH_THREE[6] * ux * (xx - 3.0 * yy),
    ]
    channels = []
    for channel in range(3):
        total = 0.5 + SH_ZERO * colors[channel]
        for k in range(1, 16):
            total = total + basis[k] * colors[3 * k + channel]
        channels.append(total)
    return [
        j_main * viewed[0] + 2048.0,
        j_main * viewed[1] + 1024.0,
        s_yy * per_det,
        -s_xy * per_det,
        s_xx * per_det,
    ] + channels


def sigmoid(value):
    return 1.0 / (1.0 + jnp.exp(-value))


def split(value):
    high = value.astype(BF16)
    rest = value - high.astype(F32)
    mid = rest.astype(BF16)
    low = (rest - mid.astype(F32)).astype(BF16)
    return high, mid, low


def pick(chooser, value):
    high, mid, low = split(value)
    return (
        jnp.dot(chooser, high, preferred_element_type=F32)
        + jnp.dot(chooser, mid, preferred_element_type=F32)
    ) + jnp.dot(chooser, low, preferred_element_type=F32)


def pick_two(chooser, value):
    high = value.astype(BF16)
    mid = (value - high.astype(F32)).astype(BF16)
    return jnp.dot(chooser, high, preferred_element_type=F32) + jnp.dot(chooser, mid, preferred_element_type=F32)


def turn(value, lanes):
    lanes = lanes % 128
    return value if lanes == 0 else pltpu.roll(value, lanes, 1)


def spread_of(first):
    lane = lax.broadcasted_iota(jnp.int32, (128, 256), 1)
    row = lax.broadcasted_iota(jnp.int32, (128, 256), 0)
    return jnp.where(row == (first + lane // 128) * 16 + lax.rem(lane, 16), 1.0, 0.0).astype(BF16)


def expand(refs, flat, wide):
    flat[56:64, :] = jnp.zeros((8, 1024), F32)
    start = 0
    for ref in refs:
        flat[start : start + ref.shape[0], :] = ref[...]
        start += ref.shape[0]
    parts = split(jnp.concatenate([flat[:, j * 128 : (j + 1) * 128] for j in range(8)], axis=0))
    for i in range(0, 8, 2):
        spread = spread_of(i)
        value = (
            jnp.dot(parts[0], spread, preferred_element_type=F32)
            + jnp.dot(parts[1], spread, preferred_element_type=F32)
        ) + jnp.dot(parts[2], spread, preferred_element_type=F32)
        wide[:, i, :] = value[:, 0:128]
        wide[:, i + 1, :] = value[:, 128:256]


def project_chunk(chunk, wide, view_ref, out):
    view = [view_ref[k] for k in range(15)]
    raw = [wide[chunk * 64 + k] for k in range(59)]
    record = screen_of(raw[0:3], covariance_of(raw[3:10]), raw[11:], view)
    slot = lax.broadcasted_iota(jnp.int32, (8, 128), 1) // 16
    rows = pl.ds(pl.multiple_of(chunk * 8, 8), 8)
    for v in range(8):
        value = turn(record[0], -v * 16)
        for k in range(1, 8):
            value = jnp.where(slot == k, turn(record[k], (k - v) * 16), value)
        out[v, rows, :] = value
    out[8, rows, :] = sigmoid(raw[10])


def place():
    return lax.axis_index("cam"), lax.axis_index("tile")


def across(c, t, i):
    index = lax.rem(c * 4 + t // 16 + i, 16)
    return (index // 4, lax.rem(index, 4) * 16 + lax.rem(t, 16))


def along(c, t, i):
    return (c, (t // 16) * 16 + lax.rem(lax.rem(t, 16) + i, 16))


def greet(c, t):
    barrier = pltpu.get_barrier_semaphore()

    def hail(i, carry):
        pl.semaphore_signal(barrier, inc=1, device_id=along(c, t, i), device_id_type=MESH)
        pl.semaphore_signal(barrier, inc=1, device_id=across(c, t, i), device_id_type=MESH)
        return carry

    lax.fori_loop(1, 16, hail, 0)
    return barrier


def send_rows(src, dst, c, t, send, recv):
    me = c * N_TILE + t

    def one(i, carry):
        to = lax.rem(me + i, N_DEV)
        pltpu.make_async_remote_copy(
            src_ref=src.at[to],
            dst_ref=dst.at[me],
            send_sem=send,
            recv_sem=recv,
            device_id=(to // N_TILE, lax.rem(to, N_TILE)),
            device_id_type=MESH,
        ).start()
        return carry

    lax.fori_loop(1, N_DEV, one, 0, unroll=5)


def send_plane(src, dst, c, t, send, recv):
    def one(i, carry):
        to = lax.rem(t + i, N_TILE)
        pltpu.make_async_remote_copy(
            src_ref=src.at[to],
            dst_ref=dst.at[t],
            send_sem=send,
            recv_sem=recv,
            device_id=(c, to),
            device_id_type=MESH,
        ).start()
        return carry

    lax.fori_loop(1, N_TILE, one, 0, unroll=3)


def send_mates(src, dst, c, t, send, recv):
    for i in range(1, N_CAM):
        pltpu.make_async_remote_copy(
            src_ref=src,
            dst_ref=dst.at[c],
            send_sem=send,
            recv_sem=recv,
            device_id=(lax.rem(c + i, N_CAM), t),
            device_id_type=MESH,
        ).start()


def wait_some(src, dst, count, send, recv):
    some = pl.ds(0, count)
    pltpu.make_async_copy(src.at[some], src.at[some], send).wait()
    pltpu.make_async_copy(dst.at[some], dst.at[some], recv).wait()


def wait_rows(src, dst, send, recv):
    most = pl.ds(0, N_DEV - 1)
    pltpu.make_async_copy(src.at[most], src.at[most], send).wait()
    pltpu.make_async_copy(dst.at[most], dst.at[most], recv).wait()


def chooser_of(table, g):
    wanted = table[g * N_TILE : (g + 1) * N_TILE, 0, :]
    lane = lax.broadcasted_iota(jnp.int32, (64, 128), 1)
    return jnp.where(wanted == lax.rem(lane, 64), 1.0, 0.0)


def main_kernel(
    place_ref,
    count_ref,
    cam,
    pos,
    scl,
    rot,
    opa,
    col,
    fetch,
    lists,
    target,
    table,
    back,
    back_o,
    mine,
    flat,
    wide,
    view_ref,
    records,
    out,
    out_o,
    data,
    data_o,
    grad,
    grad_o,
    mates,
    came_o,
    share,
    chosen,
    givers,
    spots,
    spots_o,
    cols,
    alpha_ref,
    through_ref,
    lost,
    send_a,
    recv_a,
    send_b,
    recv_b,
    send_c,
    recv_c,
    send_d,
    recv_d,
    send_g,
    recv_g,
    send_h,
    recv_h,
    send_i,
    recv_i,
    send_j,
    recv_j,
    own_a,
    own_c,
    own_d,
    own_g,
    own_h,
    own_i,
    own_j,
):
    c, t = place()
    me = c * N_TILE + t
    barrier = greet(c, t)
    block = [fetch[p, 0, 0:1, 0:1] // 16 for p in range(2)]
    half = lax.broadcasted_iota(jnp.int32, (1, 128), 1) < 64
    mine[0, :, :] = jnp.where(half, jnp.broadcast_to(block[0], (1, 128)), jnp.broadcast_to(block[1], (1, 128)))
    for k, value in enumerate(view_of(cam, lax.broadcasted_iota(jnp.int32, (8, 128), 1) // 16)):
        view_ref[k] = value
    expand((pos, scl, rot, opa, col), flat, wide)

    def step(chunk, carry):
        project_chunk(chunk, wide, view_ref, records)
        return carry

    local = pltpu.make_async_copy(mine.at[0], table.at[me], own_a)
    local.start()
    pl.semaphore_wait(barrier, 30)

    def first(i, carry):
        pltpu.make_async_remote_copy(
            src_ref=mine.at[0],
            dst_ref=table.at[me],
            send_sem=send_a,
            recv_sem=recv_a,
            device_id=along(c, t, i),
            device_id_type=MESH,
        ).start()
        return carry

    lax.fori_loop(1, 16, first, 0)
    lax.fori_loop(0, 8, step, 0)
    local_o = pltpu.make_async_copy(records.at[8], mates.at[c], own_g)
    local_o.start()
    send_mates(records.at[8], mates, c, t, send_g, recv_g)
    local.wait()
    some = pl.ds(0, 15)
    pltpu.make_async_copy(table.at[some], table.at[some], send_a).wait()
    pltpu.make_async_copy(table.at[some], table.at[some], recv_a).wait()
    line = pl.ds(c * N_TILE + (t // 16) * 16, 16)

    def second(i, carry):
        pltpu.make_async_remote_copy(
            src_ref=table.at[line],
            dst_ref=table.at[line],
            send_sem=send_b,
            recv_sem=recv_b,
            device_id=across(c, t, i),
            device_id_type=MESH,
        ).start()
        return carry

    lax.fori_loop(1, 16, second, 0)
    for p in range(2):
        prepare(p, fetch, lists, chosen, givers, spots, spots_o)
    most = pl.ds(0, 240)
    pltpu.make_async_copy(table.at[most], table.at[most], send_b).wait()
    pltpu.make_async_copy(table.at[most], table.at[most], recv_b).wait()

    lane = lax.broadcasted_iota(jnp.int32, (64, 128), 1)
    even = lax.rem(lane // 16, 2) == 0
    local_o.wait()
    wait_some(mates, mates, 3, send_g, recv_g)
    opacity = mates[0]
    for g in range(1, N_CAM):
        opacity = jnp.where(lane // 32 == g, mates[g], opacity)
    opacity = jnp.concatenate([jnp.where(even, opacity, 0.0), jnp.where(even, 0.0, opacity)], axis=0)
    mine_rows = pl.ds(c * N_TILE, N_TILE)
    chooser = jnp.where(table[mine_rows, 0, :] == lax.rem(lane, 64), 1.0, 0.0)
    turned = chooser.T.astype(BF16)
    out_o[:, 0, :] = pick(chooser.astype(BF16), opacity)
    local_o = pltpu.make_async_copy(out_o.at[t], data_o.at[t], own_h)
    local_o.start()
    send_plane(out_o, data_o, c, t, send_h, recv_h)
    none = jnp.zeros((64, 128), F32)
    for g in range(N_CAM):
        chooser = chooser_of(table, g).astype(BF16)
        upper = jnp.concatenate([records[2 * g], none], axis=1)
        lower = jnp.concatenate([none, records[2 * g + 1]], axis=1)
        value = pick(chooser, jnp.concatenate([upper, lower], axis=0))
        here = pl.ds(g * N_TILE, N_TILE)
        out[here, 0, :] = value[:, 0:128]
        out[here, 1, :] = value[:, 128:256]
    local = pltpu.make_async_copy(out.at[me], data.at[me], own_c)
    local.start()
    send_rows(out, data, c, t, send_c, recv_c)
    local_o.wait()
    wait_some(out_o, data_o, N_TILE - 1, send_h, recv_h)
    local.wait()
    wait_rows(out, data, send_c, recv_c)
    shared = (place_ref, count_ref, chosen, givers, spots, spots_o, target, cols, alpha_ref, through_ref, lost)
    for p in range(2):
        opacity = jnp.concatenate([data_o[:, 0, :]] * N_CAM, axis=0)
        given, given_o = render(p, data[:, p, :], opacity, *shared)
        grad[:, p, :] = given
        grad_o[:, 0, :] = given_o if p == 0 else grad_o[:, 0, :] + given_o
    local_o = pltpu.make_async_copy(grad_o.at[t], came_o.at[t], own_i)
    local_o.start()
    send_plane(grad_o, came_o, c, t, send_i, recv_i)
    local = pltpu.make_async_copy(grad.at[me], back.at[me], own_d)
    local.start()
    send_rows(grad, back, c, t, send_d, recv_d)
    local_o.wait()
    wait_some(grad_o, came_o, N_TILE - 1, send_i, recv_i)
    both = pick_two(turned, came_o[:, 0, :])
    share[...] = jnp.where(even, both[0:64], both[64:128])
    local_o = pltpu.make_async_copy(share, back_o.at[c], own_j)
    local_o.start()
    send_mates(share, back_o, c, t, send_j, recv_j)
    local_o.wait()
    wait_some(back_o, back_o, 3, send_j, recv_j)
    local.wait()
    wait_rows(grad, back, send_d, recv_d)


def prepare(p, fetch, lists, chosen, givers, spots, spots_o):
    wide = lax.broadcasted_iota(jnp.int32, (LIST, N_DEV), 1)
    tall = lax.broadcasted_iota(jnp.int32, (LIST, N_DEV), 0)
    listed = jnp.broadcast_to(lists[p], (LIST, N_DEV)).astype(F32)
    slot = jnp.sum(jnp.where(wide == lax.rem(tall, 8) * 32 + tall // 8, listed, 0.0), axis=1, keepdims=True)
    slot = slot.astype(jnp.int32)
    chooser = jnp.where(wide == slot // 8, 1.0, 0.0)
    givers[p] = chooser.T.astype(BF16)
    chooser = chooser.astype(BF16)
    chosen[p] = chooser
    within = jnp.concatenate([lax.rem(fetch[p, g], 16).astype(F32) for g in range(N_CAM)], axis=1).astype(BF16)
    near = lax.dot_general(chooser, within, (((1,), (1,)), ((), ())), preferred_element_type=F32)
    eight = lax.broadcasted_iota(jnp.int32, near.shape, 1)
    column = jnp.sum(jnp.where(eight == lax.rem(slot, 8), near, 0.0), axis=1, keepdims=True)
    spot = jnp.broadcast_to(column, (LIST, 128)).astype(jnp.int32)
    spots[p] = spot
    spots_o[p] = spot + (slot // 512) * 32 + p * 16


def before_of(run):
    row = lax.broadcasted_iota(jnp.int32, (8, 128), 0)
    for s in (1, 2, 4):
        run = run * jnp.where(row >= s, pltpu.roll(run, s, 0), 1.0)
    return jnp.where(row >= 1, pltpu.roll(run, 1, 0), 1.0)


def after_of(run):
    row = lax.broadcasted_iota(jnp.int32, (8, 128), 0)
    for s in (1, 2, 4):
        run = run + jnp.where(row < 8 - s, pltpu.roll(run, 8 - s, 0), 0.0)
    return jnp.where(row < 7, pltpu.roll(run, 7, 0), 0.0)


def render(
    p, data, opacity, place_ref, count_ref, chosen, givers, spots, spots_o, target, cols, alpha_ref, through_ref, lost
):
    lane_b = lax.broadcasted_iota(jnp.int32, (BLK, 128), 1)
    row_b = lax.broadcasted_iota(jnp.int32, (BLK, 128), 0)
    lane_1 = lax.broadcasted_iota(jnp.int32, (1, 128), 1)
    blocks, parts = LIST // BLK, BLK // 8
    picked = pick(chosen[p], jnp.concatenate([data, opacity], axis=1))
    spot = spots[p]
    for k in range(8):
        cols[k] = jnp.take_along_axis(picked[:, 0:128], spot + k * 16, axis=1)
    cols[8] = jnp.take_along_axis(picked[:, 128:256], spots_o[p], axis=1)

    tile = place_ref[p]
    count = count_ref[p]
    left = (lax.rem(tile, 256) * 16).astype(F32) + 0.5
    top = ((tile // 256) * 16).astype(F32) + 0.5
    px = left + lax.rem(lane_1, 16).astype(F32)
    py = [top + ((lane_1 + h * 128) // 16).astype(F32) for h in range(2)]

    def ahead(b, carry):
        rows = pl.ds(pl.multiple_of(b * BLK, BLK), BLK)
        u, v, ca, cb, cc = [cols[k, rows, :] for k in range(5)]
        shade = [cols[k, rows, :] for k in (5, 6, 7)]
        o = cols[8, rows, :]
        live = lax.rem(row_b, 8) * 32 + row_b // 8 + b * parts < count
        dx = px - u
        dxx = ca * dx * dx
        result = []
        for h in range(2):
            run, shown = carry[h][0], list(carry[h][1:])
            dy = py[h] - v
            quad = dxx + 2.0 * cb * dx * dy + cc * dy * dy
            alpha = jnp.where(live, o * jnp.exp(-0.5 * quad), 0.0)
            alpha_ref[h, rows, :] = alpha
            keep = 1.0 - alpha
            before = []
            for n in range(parts):
                before.append(run)
                run = run * keep[8 * n : 8 * n + 8]
            before = jnp.concatenate(before, axis=0)
            through_ref[h, rows, :] = before
            weight = alpha * before
            for k in range(3):
                value = shade[k] * weight
                for n in range(parts):
                    shown[k] = shown[k] + value[8 * n : 8 * n + 8]
            result.append((run, *shown))
        return tuple(result)

    one, zero = jnp.ones((8, 128), F32), jnp.zeros((8, 128), F32)
    state = lax.fori_loop(0, blocks, ahead, ((one, zero, zero, zero),) * 2)
    ahead_of, miss, behind = [], [], []
    for h in range(2):
        prefix = before_of(state[h][0])
        parts_of = [prefix * state[h][1 + k] for k in range(3)]
        gap = [
            jnp.sum(parts_of[k], axis=0, keepdims=True) - target[p, k, :, h * 128 : (h + 1) * 128]
            for k in range(3)
        ]
        ahead_of.append(jnp.concatenate([prefix] * parts, axis=0))
        miss.append(gap)
        behind.append(after_of(gap[0] * parts_of[0] + gap[1] * parts_of[1] + gap[2] * parts_of[2]))

    def back(i, carry):
        b = blocks - 1 - i
        rows = pl.ds(pl.multiple_of(b * BLK, BLK), BLK)
        u, v, ca, cb, cc = [cols[k, rows, :] for k in range(5)]
        shade = [cols[k, rows, :] for k in (5, 6, 7)]
        o = cols[8, rows, :]
        dx = px - u
        sums = [0.0] * 9
        result = []
        for h in range(2):
            alpha = alpha_ref[h, rows, :]
            before = through_ref[h, rows, :] * ahead_of[h]
            dy = py[h] - v
            weight = alpha * before
            pull = shade[0] * miss[h][0] + shade[1] * miss[h][1] + shade[2] * miss[h][2]
            value = pull * weight
            run = carry[h]
            after = []
            for n in reversed(range(parts)):
                after.insert(0, run)
                run = run + value[8 * n : 8 * n + 8]
            result.append(run)
            after = jnp.concatenate(after, axis=0)
            slope = (before * pull - after / (1.0 - alpha)) * alpha
            tilt_x, tilt_y = slope * dx, slope * dy
            terms = [tilt_x, tilt_y, tilt_x * dx, tilt_x * dy, tilt_y * dy, slope]
            terms = terms + [weight * miss[h][k] for k in range(3)]
            sums = [x + y for x, y in zip(sums, terms)]
        m_x, m_y, m_xx, m_xy, m_yy, m_0, *g_shade = [jnp.sum(x, axis=1, keepdims=True) for x in sums]
        grads = [ca * m_x + cb * m_y, cb * m_x + cc * m_y, -0.5 * m_xx, -m_xy, -0.5 * m_yy] + g_shade
        spot_b = spots[p, rows, :]
        value = jnp.zeros((BLK, 128), F32)
        for k in range(8):
            value = jnp.where(lane_b == spot_b + k * 16, jnp.broadcast_to(grads[k], (BLK, 128)), value)
        lost[rows, 0:128] = value
        lost[rows, 128:256] = jnp.where(lane_b == spots_o[p, rows, :], m_0 / o, 0.0)
        return tuple(result)

    lax.fori_loop(0, blocks, back, tuple(behind))
    given = pick_two(givers[p], lost[...])
    by_tile = given[0:64, 128:256]
    for g in range(1, N_CAM):
        by_tile = by_tile + given[g * 64 : g * 64 + 64, 128:256]
    return given[:, 0:128], by_tile


def gradient_kernel(
    cam, pos, scl, rot, opa, col, table, back, back_o, g_pos, g_scl, g_rot, g_opa, g_col, raw, view_ref, cot, total
):
    row = lax.broadcasted_iota(jnp.int32, (8, 128), 0)
    lane = lax.broadcasted_iota(jnp.int32, (8, 128), 1)
    for k, value in enumerate(view_of(cam, row)):
        view_ref[k] = value
    start = 0
    for ref in (pos, scl, rot, opa, col):
        for j in range(8):
            raw[start : start + ref.shape[0], j, :] = ref[:, j * 128 : (j + 1) * 128]
        start += ref.shape[0]

    def fold(value, first):
        out = jnp.zeros((8, 128), F32)
        for j in range(8):
            part = jnp.take_along_axis(value[8 * j : 8 * j + 8], first + lax.rem(lane, 16), axis=1)
            part = jnp.take_along_axis(part, lane // 16, axis=0)
            out = jnp.where(row == j, part, out)
        return out

    own = lax.axis_index("cam") * 32
    shared = (back_o[0] + back_o[1]) + (back_o[2] + back_o[3])
    opacity = fold(shared, own) + fold(shared, own + 16)
    for g in range(N_CAM):
        chooser = chooser_of(table, g).T.astype(BF16)
        here = pl.ds(g * N_TILE, N_TILE)
        sent = jnp.concatenate([back[here, 0, :], back[here, 1, :]], axis=1)
        value = pick_two(chooser, sent)
        for p in range(2):
            part = value[p * 64 : p * 64 + 64, p * 128 : p * 128 + 128]
            for v in range(8):
                cot[2 * g + p, v] = fold(part, v * 16)
    for k in range(57):
        total[k] = jnp.zeros((8, 128), F32)
    shape_raw = [raw[k] for k in range(3, 10)]
    for k, value in enumerate(covariance_of(shape_raw)):
        cot[8, k] = value

    def step(v, carry):
        view = [view_ref[k, pl.ds(v, 1), :] for k in range(15)]
        point = [raw[k] for k in range(3)]
        cov = [cot[8, k] for k in range(6)]
        colors = [raw[11 + k] for k in range(48)]
        _, pull = jax.vjp(lambda a, b, d: screen_of(a, b, d, view), point, cov, colors)
        grads = pull([cot[v, k] for k in range(8)])
        for k, value in enumerate(grads[0] + grads[1] + grads[2]):
            total[k] = total[k] + value
        return carry

    lax.fori_loop(0, 8, step, 0)
    _, pull = jax.vjp(covariance_of, [raw[k] for k in range(3, 10)])
    (shape_grads,) = pull([total[3 + k] for k in range(6)])
    for k in range(7):
        total[57 + k] = shape_grads[k]
    o = sigmoid(raw[10])
    total[3] = opacity * o * (1.0 - o)
    for j in range(8):
        here = pl.ds(j * 128, 128)
        g_pos[:, here] = total[0:3, j, :]
        g_scl[:, here] = total[57:60, j, :]
        g_rot[:, here] = total[60:64, j, :]
        g_opa[:, here] = total[3:4, j, :]
        g_col[:, here] = total[9:57, j, :]


VMEM = pl.BlockSpec(memory_space=pltpu.VMEM)
SMEM = pl.BlockSpec(memory_space=pltpu.SMEM)
DMA = pltpu.SemaphoreType.DMA


def shape(*dims, dtype=F32):
    return jax.ShapeDtypeStruct(dims, dtype)


def body(
    positions,
    log_scales,
    rotations,
    opacities,
    colors,
    cameras,
    targets,
    tile_ids,
    tile_counts,
    tile_lists,
    fetch_ids,
):
    params = (positions, log_scales, rotations, opacities.reshape(1, 1024), colors)
    whole, plane = pltpu.VMEM((N_DEV, 2, 128), F32), pltpu.VMEM((N_TILE, 1, 128), F32)
    table, back, back_o = pl.pallas_call(
        main_kernel,
        out_shape=(
            shape(N_DEV, 1, 128, dtype=jnp.int32),
            shape(N_DEV, 2, 128),
            shape(N_CAM, 64, 128),
        ),
        in_specs=[SMEM] * 3 + [VMEM] * 8,
        out_specs=(VMEM,) * 3,
        scratch_shapes=[
            pltpu.VMEM((1, 1, 128), jnp.int32),
            pltpu.VMEM((64, 1024), F32),
            pltpu.VMEM((512, 8, 128), F32),
            pltpu.VMEM((15, 8, 128), F32),
            pltpu.VMEM((9, 64, 128), F32),
            whole,
            plane,
            whole,
            plane,
            whole,
            plane,
            pltpu.VMEM((N_CAM, 64, 128), F32),
            plane,
            pltpu.VMEM((64, 128), F32),
            pltpu.VMEM((2, LIST, N_DEV), BF16),
            pltpu.VMEM((2, N_DEV, LIST), BF16),
            pltpu.VMEM((2, LIST, 128), jnp.int32),
            pltpu.VMEM((2, LIST, 128), jnp.int32),
            pltpu.VMEM((9, LIST, 128), F32),
            pltpu.VMEM((2, LIST, 128), F32),
            pltpu.VMEM((2, LIST, 128), F32),
            pltpu.VMEM((LIST, 2 * 128), F32),
        ]
        + [DMA] * 23,
        compiler_params=pltpu.CompilerParams(collective_id=0, has_side_effects=True),
    )(
        tile_ids.reshape(2),
        tile_counts.reshape(2),
        cameras,
        *params,
        fetch_ids.reshape(2, N_CAM, N_TILE, 8).transpose(0, 1, 3, 2),
        tile_lists.reshape(2, 1, LIST),
        targets.reshape(2, 3, 1, PIX),
    )

    g_pos, g_scl, g_rot, g_opa, g_col = pl.pallas_call(
        gradient_kernel,
        out_shape=tuple(shape(n, 1024) for n in (3, 3, 4, 1, 48)),
        in_specs=[SMEM] + [VMEM] * 8,
        out_specs=(VMEM,) * 5,
        scratch_shapes=[
            pltpu.VMEM((59, 8, 128), F32),
            pltpu.VMEM((15, 8, 128), F32),
            pltpu.VMEM((9, 8, 8, 128), F32),
            pltpu.VMEM((64, 8, 128), F32),
        ],
    )(cameras, *params, table, back, back_o)
    return g_pos, g_scl, g_rot, g_opa.reshape(1024), g_col


def solution(mesh):
    return jax.shard_map(
        body,
        mesh=mesh,
        in_specs=(
            P(None, ("cam", "tile")),
            P(None, ("cam", "tile")),
            P(None, ("cam", "tile")),
            P(("cam", "tile")),
            P(None, ("cam", "tile")),
            P(),
            P(None, "cam", "tile", None, None),
            P(None, "cam", "tile"),
            P(None, "cam", "tile"),
            P(None, "cam", "tile", None),
            P(None, "cam", "tile", None, None, None),
        ),
        out_specs=(
            P(None, ("cam", "tile")),
            P(None, ("cam", "tile")),
            P(None, ("cam", "tile")),
            P(("cam", "tile")),
            P(None, ("cam", "tile")),
        ),
        check_vma=False,
    )
```

```python
import jax
import jax.numpy as jnp
from jax import lax
from jax.experimental import pallas as pl
from jax.experimental.pallas import tpu as pltpu
from jax.sharding import PartitionSpec as P

N_CAM, N_TILE, N_DEV = 4, 64, 256
LIST, PIX, BLK = 256, 256, 32
MESH = pl.DeviceIdType.MESH
F32, BF16 = jnp.float32, jnp.bfloat16

FOCAL = 4096.0
SH_ZERO = 0.28209479177387814
SH_ONE = 0.4886025119029199
SH_TWO = [
    1.0925484305920792,
    -1.0925484305920792,
    0.31539156525252005,
    -1.0925484305920792,
    0.5462742152960396,
]
SH_THREE = [
    -0.5900435899266435,
    2.890611442640554,
    -0.4570457994644658,
    0.3731763325901154,
    -0.4570457994644658,
    1.445305721320277,
    -0.5900435899266435,
]


def matmul3(left, right):
    return [
        [
            left[i][0] * right[0][j] + left[i][1] * right[1][j] + left[i][2] * right[2][j]
            for j in range(3)
        ]
        for i in range(3)
    ]


def view_of(cam_ref, view):
    values = []
    for k in range(6):
        value = jnp.zeros((8, 128), F32)
        for c in range(N_CAM):
            for p in range(2):
                value = jnp.where(view == c * 2 + p, cam_ref[p, c, k], value)
        values.append(value)
    cos_a, sin_a = jnp.cos(values[0]), jnp.sin(values[0])
    cos_b, sin_b = jnp.cos(values[1]), jnp.sin(values[1])
    cos_c, sin_c = jnp.cos(values[2]), jnp.sin(values[2])
    rotate = [
        [cos_c * cos_b, cos_c * sin_b * sin_a - sin_c * cos_a, cos_c * sin_b * cos_a + sin_c * sin_a],
        [sin_c * cos_b, sin_c * sin_b * sin_a + cos_c * cos_a, sin_c * sin_b * cos_a - cos_c * sin_a],
        [-sin_b, cos_b * sin_a, cos_b * cos_a],
    ]
    offset = [values[3], values[4], 6.0 + values[5]]
    anchor = [
        -(rotate[0][j] * offset[0] + rotate[1][j] * offset[1] + rotate[2][j] * offset[2])
        for j in range(3)
    ]
    return [rotate[i][j] for i in range(3) for j in range(3)] + offset + anchor


def covariance_of(raw):
    quat_norm = jnp.sqrt(raw[3] * raw[3] + raw[4] * raw[4] + raw[5] * raw[5] + raw[6] * raw[6])
    per_norm = 1.0 / quat_norm
    qw, qx, qy, qz = (raw[3] * per_norm, raw[4] * per_norm, raw[5] * per_norm, raw[6] * per_norm)
    spin = [
        [1.0 - 2.0 * (qy * qy + qz * qz), 2.0 * (qx * qy - qw * qz), 2.0 * (qx * qz + qw * qy)],
        [2.0 * (qx * qy + qw * qz), 1.0 - 2.0 * (qx * qx + qz * qz), 2.0 * (qy * qz - qw * qx)],
        [2.0 * (qx * qz - qw * qy), 2.0 * (qy * qz + qw * qx), 1.0 - 2.0 * (qx * qx + qy * qy)],
    ]
    squares = [jnp.exp(2.0 * raw[k]) for k in range(3)]
    return [
        spin[i][0] * spin[j][0] * squares[0]
        + spin[i][1] * spin[j][1] * squares[1]
        + spin[i][2] * spin[j][2] * squares[2]
        for i, j in ((0, 0), (0, 1), (0, 2), (1, 1), (1, 2), (2, 2))
    ]


def screen_of(point, cov, colors, view):
    rotate = [view[0:3], view[3:6], view[6:9]]
    offset, anchor = view[9:12], view[12:15]
    viewed = [
        rotate[i][0] * point[0] + rotate[i][1] * point[1] + rotate[i][2] * point[2] + offset[i]
        for i in range(3)
    ]
    toward = [point[j] - anchor[j] for j in range(3)]
    length = jnp.sqrt(toward[0] * toward[0] + toward[1] * toward[1] + toward[2] * toward[2])
    per_length = 1.0 / length
    ux, uy, uz = (toward[0] * per_length, toward[1] * per_length, toward[2] * per_length)
    world = [[cov[0], cov[1], cov[2]], [cov[1], cov[3], cov[4]], [cov[2], cov[4], cov[5]]]
    half_way = matmul3(rotate, world)

    def seen(a, b):
        return (
            half_way[a][0] * rotate[b][0] + half_way[a][1] * rotate[b][1] + half_way[a][2] * rotate[b][2]
        )

    c00, c01, c02 = seen(0, 0), seen(0, 1), seen(0, 2)
    c11, c12, c22 = seen(1, 1), seen(1, 2), seen(2, 2)
    inverse = 1.0 / viewed[2]
    j_main = FOCAL * inverse
    j_side_x = -j_main * viewed[0] * inverse
    j_side_y = -j_main * viewed[1] * inverse
    s_xx = j_main * j_main * c00 + 2.0 * j_main * j_side_x * c02 + j_side_x * j_side_x * c22 + 0.3
    s_xy = (
        j_main * j_main * c01
        + j_main * j_side_y * c02
        + j_side_x * j_main * c12
        + j_side_x * j_side_y * c22
    )
    s_yy = j_main * j_main * c11 + 2.0 * j_main * j_side_y * c12 + j_side_y * j_side_y * c22 + 0.3
    per_det = 1.0 / (s_xx * s_yy - s_xy * s_xy)
    xx, yy, zz = (ux * ux, uy * uy, uz * uz)
    basis = [
        None,
        -SH_ONE * uy,
        SH_ONE * uz,
        -SH_ONE * ux,
        SH_TWO[0] * ux * uy,
        SH_TWO[1] * uy * uz,
        SH_TWO[2] * (2.0 * zz - xx - yy),
        SH_TWO[3] * ux * uz,
        SH_TWO[4] * (xx - yy),
        SH_THREE[0] * uy * (3.0 * xx - yy),
        SH_THREE[1] * ux * uy * uz,
        SH_THREE[2] * uy * (4.0 * zz - xx - yy),
        SH_THREE[3] * uz * (2.0 * zz - 3.0 * xx - 3.0 * yy),
        SH_THREE[4] * ux * (4.0 * zz - xx - yy),
        SH_THREE[5] * uz * (xx - yy),
        SH_THREE[6] * ux * (xx - 3.0 * yy),
    ]
    channels = []
    for channel in range(3):
        total = 0.5 + SH_ZERO * colors[channel]
        for k in range(1, 16):
            total = total + basis[k] * colors[3 * k + channel]
        channels.append(total)
    return [
        j_main * viewed[0] + 2048.0,
        j_main * viewed[1] + 1024.0,
        s_yy * per_det,
        -s_xy * per_det,
        s_xx * per_det,
    ] + channels


def sigmoid(value):
    return 1.0 / (1.0 + jnp.exp(-value))


def split(value):
    high = value.astype(BF16)
    rest = value - high.astype(F32)
    mid = rest.astype(BF16)
    low = (rest - mid.astype(F32)).astype(BF16)
    return high, mid, low


def pick(chooser, value):
    high, mid, low = split(value)
    return (
        jnp.dot(chooser, high, preferred_element_type=F32)
        + jnp.dot(chooser, mid, preferred_element_type=F32)
    ) + jnp.dot(chooser, low, preferred_element_type=F32)


def pick_two(chooser, value):
    high = value.astype(BF16)
    mid = (value - high.astype(F32)).astype(BF16)
    return jnp.dot(chooser, high, preferred_element_type=F32) + jnp.dot(chooser, mid, preferred_element_type=F32)


def turn(value, lanes):
    lanes = lanes % 128
    return value if lanes == 0 else pltpu.roll(value, lanes, 1)


def spread_of(first):
    lane = lax.broadcasted_iota(jnp.int32, (128, 256), 1)
    row = lax.broadcasted_iota(jnp.int32, (128, 256), 0)
    return jnp.where(row == (first + lane // 128) * 16 + lax.rem(lane, 16), 1.0, 0.0).astype(BF16)


def expand(refs, flat, wide):
    flat[56:64, :] = jnp.zeros((8, 1024), F32)
    start = 0
    for ref in refs:
        flat[start : start + ref.shape[0], :] = ref[...]
        start += ref.shape[0]
    parts = split(jnp.concatenate([flat[:, j * 128 : (j + 1) * 128] for j in range(8)], axis=0))
    for i in range(0, 8, 2):
        spread = spread_of(i)
        value = (
            jnp.dot(parts[0], spread, preferred_element_type=F32)
            + jnp.dot(parts[1], spread, preferred_element_type=F32)
        ) + jnp.dot(parts[2], spread, preferred_element_type=F32)
        wide[:, i, :] = value[:, 0:128]
        wide[:, i + 1, :] = value[:, 128:256]


def project_chunk(chunk, wide, view_ref, out):
    view = [view_ref[k] for k in range(15)]
    raw = [wide[chunk * 64 + k] for k in range(59)]
    record = screen_of(raw[0:3], covariance_of(raw[3:10]), raw[11:], view)
    slot = lax.broadcasted_iota(jnp.int32, (8, 128), 1) // 16
    rows = pl.ds(pl.multiple_of(chunk * 8, 8), 8)
    for v in range(8):
        value = turn(record[0], -v * 16)
        for k in range(1, 8):
            value = jnp.where(slot == k, turn(record[k], (k - v) * 16), value)
        out[v, rows, :] = value
    out[8, rows, :] = sigmoid(raw[10])


def place():
    return lax.axis_index("cam"), lax.axis_index("tile")


def across(c, t, i):
    index = lax.rem(c * 4 + t // 16 + i, 16)
    return (index // 4, lax.rem(index, 4) * 16 + lax.rem(t, 16))


def along(c, t, i):
    return (c, (t // 16) * 16 + lax.rem(lax.rem(t, 16) + i, 16))


def greet(c, t):
    barrier = pltpu.get_barrier_semaphore()

    def hail(i, carry):
        pl.semaphore_signal(barrier, inc=1, device_id=along(c, t, i), device_id_type=MESH)
        pl.semaphore_signal(barrier, inc=1, device_id=across(c, t, i), device_id_type=MESH)
        return carry

    lax.fori_loop(1, 16, hail, 0)
    return barrier


def send_rows(src, dst, c, t, send, recv):
    me = c * N_TILE + t

    def one(i, carry):
        to = lax.rem(me + i, N_DEV)
        pltpu.make_async_remote_copy(
            src_ref=src.at[to],
            dst_ref=dst.at[me],
            send_sem=send,
            recv_sem=recv,
            device_id=(to // N_TILE, lax.rem(to, N_TILE)),
            device_id_type=MESH,
        ).start()
        return carry

    lax.fori_loop(1, N_DEV, one, 0, unroll=5)


def send_plane(src, dst, c, t, send, recv):
    def one(i, carry):
        to = lax.rem(t + i, N_TILE)
        pltpu.make_async_remote_copy(
            src_ref=src.at[to],
            dst_ref=dst.at[t],
            send_sem=send,
            recv_sem=recv,
            device_id=(c, to),
            device_id_type=MESH,
        ).start()
        return carry

    lax.fori_loop(1, N_TILE, one, 0, unroll=3)


def send_mates(src, dst, c, t, send, recv):
    for i in range(1, N_CAM):
        pltpu.make_async_remote_copy(
            src_ref=src,
            dst_ref=dst.at[c],
            send_sem=send,
            recv_sem=recv,
            device_id=(lax.rem(c + i, N_CAM), t),
            device_id_type=MESH,
        ).start()


def wait_some(src, dst, count, send, recv):
    some = pl.ds(0, count)
    pltpu.make_async_copy(src.at[some], src.at[some], send).wait()
    pltpu.make_async_copy(dst.at[some], dst.at[some], recv).wait()


def wait_rows(src, dst, send, recv):
    most = pl.ds(0, N_DEV - 1)
    pltpu.make_async_copy(src.at[most], src.at[most], send).wait()
    pltpu.make_async_copy(dst.at[most], dst.at[most], recv).wait()


def chooser_of(table, g):
    wanted = table[g * N_TILE : (g + 1) * N_TILE, 0, :]
    lane = lax.broadcasted_iota(jnp.int32, (64, 128), 1)
    return jnp.where(wanted == lax.rem(lane, 64), 1.0, 0.0)


def main_kernel(
    place_ref,
    count_ref,
    cam,
    far_pos,
    far_scl,
    far_rot,
    far_opa,
    far_col,
    far_fetch,
    far_lists,
    far_target,
    table,
    back,
    back_o,
    pos,
    scl,
    rot,
    opa,
    col,
    fetch,
    lists,
    target,
    mine,
    flat,
    wide,
    view_ref,
    records,
    out,
    out_o,
    data,
    data_o,
    grad,
    grad_o,
    mates,
    came_o,
    share,
    chosen,
    givers,
    spots,
    spots_o,
    cols,
    alpha_ref,
    through_ref,
    lost,
    send_a,
    recv_a,
    send_b,
    recv_b,
    send_c,
    recv_c,
    send_d,
    recv_d,
    send_g,
    recv_g,
    send_h,
    recv_h,
    send_i,
    recv_i,
    send_j,
    recv_j,
    own_a,
    own_c,
    own_d,
    own_g,
    own_h,
    own_i,
    own_j,
    loads,
):
    c, t = place()
    me = c * N_TILE + t
    fars = (far_pos, far_scl, far_rot, far_opa, far_col, far_fetch, far_lists, far_target)
    nears = (pos, scl, rot, opa, col, fetch, lists, target)
    copies = [pltpu.make_async_copy(far, near, loads.at[k]) for k, (far, near) in enumerate(zip(fars, nears))]
    for copy in copies:
        copy.start()
    barrier = greet(c, t)
    for k, value in enumerate(view_of(cam, lax.broadcasted_iota(jnp.int32, (8, 128), 1) // 16)):
        view_ref[k] = value
    for copy in copies:
        copy.wait()
    block = [fetch[p, 0, 0:1, 0:1] // 16 for p in range(2)]
    half = lax.broadcasted_iota(jnp.int32, (1, 128), 1) < 64
    mine[0, :, :] = jnp.where(half, jnp.broadcast_to(block[0], (1, 128)), jnp.broadcast_to(block[1], (1, 128)))
    expand((pos, scl, rot, opa, col), flat, wide)

    def step(chunk, carry):
        project_chunk(chunk, wide, view_ref, records)
        return carry

    local = pltpu.make_async_copy(mine.at[0], table.at[me], own_a)
    local.start()
    pl.semaphore_wait(barrier, 30)

    def first(i, carry):
        pltpu.make_async_remote_copy(
            src_ref=mine.at[0],
            dst_ref=table.at[me],
            send_sem=send_a,
            recv_sem=recv_a,
            device_id=along(c, t, i),
            device_id_type=MESH,
        ).start()
        return carry

    lax.fori_loop(1, 16, first, 0)
    lax.fori_loop(0, 8, step, 0)
    local_o = pltpu.make_async_copy(records.at[8], mates.at[c], own_g)
    local_o.start()
    send_mates(records.at[8], mates, c, t, send_g, recv_g)
    local.wait()
    some = pl.ds(0, 15)
    pltpu.make_async_copy(table.at[some], table.at[some], send_a).wait()
    pltpu.make_async_copy(table.at[some], table.at[some], recv_a).wait()
    line = pl.ds(c * N_TILE + (t // 16) * 16, 16)

    def second(i, carry):
        pltpu.make_async_remote_copy(
            src_ref=table.at[line],
            dst_ref=table.at[line],
            send_sem=send_b,
            recv_sem=recv_b,
            device_id=across(c, t, i),
            device_id_type=MESH,
        ).start()
        return carry

    lax.fori_loop(1, 16, second, 0)
    for p in range(2):
        prepare(p, fetch, lists, chosen, givers, spots, spots_o)
    most = pl.ds(0, 240)
    pltpu.make_async_copy(table.at[most], table.at[most], send_b).wait()
    pltpu.make_async_copy(table.at[most], table.at[most], recv_b).wait()

    lane = lax.broadcasted_iota(jnp.int32, (64, 128), 1)
    even = lax.rem(lane // 16, 2) == 0
    local_o.wait()
    wait_some(mates, mates, 3, send_g, recv_g)
    opacity = mates[0]
    for g in range(1, N_CAM):
        opacity = jnp.where(lane // 32 == g, mates[g], opacity)
    opacity = jnp.concatenate([jnp.where(even, opacity, 0.0), jnp.where(even, 0.0, opacity)], axis=0)
    mine_rows = pl.ds(c * N_TILE, N_TILE)
    chooser = jnp.where(table[mine_rows, 0, :] == lax.rem(lane, 64), 1.0, 0.0)
    turned = chooser.T.astype(BF16)
    out_o[:, 0, :] = pick(chooser.astype(BF16), opacity)
    local_o = pltpu.make_async_copy(out_o.at[t], data_o.at[t], own_h)
    local_o.start()
    send_plane(out_o, data_o, c, t, send_h, recv_h)
    none = jnp.zeros((64, 128), F32)
    for g in range(N_CAM):
        chooser = chooser_of(table, g).astype(BF16)
        upper = jnp.concatenate([records[2 * g], none], axis=1)
        lower = jnp.concatenate([none, records[2 * g + 1]], axis=1)
        value = pick(chooser, jnp.concatenate([upper, lower], axis=0))
        here = pl.ds(g * N_TILE, N_TILE)
        out[here, 0, :] = value[:, 0:128]
        out[here, 1, :] = value[:, 128:256]
    local = pltpu.make_async_copy(out.at[me], data.at[me], own_c)
    local.start()
    send_rows(out, data, c, t, send_c, recv_c)
    local_o.wait()
    wait_some(out_o, data_o, N_TILE - 1, send_h, recv_h)
    local.wait()
    wait_rows(out, data, send_c, recv_c)
    shared = (place_ref, count_ref, chosen, givers, spots, spots_o, target, cols, alpha_ref, through_ref, lost)
    for p in range(2):
        opacity = jnp.concatenate([data_o[:, 0, :]] * N_CAM, axis=0)
        given, given_o = render(p, data[:, p, :], opacity, *shared)
        grad[:, p, :] = given
        grad_o[:, 0, :] = given_o if p == 0 else grad_o[:, 0, :] + given_o
    local_o = pltpu.make_async_copy(grad_o.at[t], came_o.at[t], own_i)
    local_o.start()
    send_plane(grad_o, came_o, c, t, send_i, recv_i)
    local = pltpu.make_async_copy(grad.at[me], back.at[me], own_d)
    local.start()
    send_rows(grad, back, c, t, send_d, recv_d)
    local_o.wait()
    wait_some(grad_o, came_o, N_TILE - 1, send_i, recv_i)
    both = pick_two(turned, came_o[:, 0, :])
    share[...] = jnp.where(even, both[0:64], both[64:128])
    local_o = pltpu.make_async_copy(share, back_o.at[c], own_j)
    local_o.start()
    send_mates(share, back_o, c, t, send_j, recv_j)
    local_o.wait()
    wait_some(back_o, back_o, 3, send_j, recv_j)
    local.wait()
    wait_rows(grad, back, send_d, recv_d)


def prepare(p, fetch, lists, chosen, givers, spots, spots_o):
    wide = lax.broadcasted_iota(jnp.int32, (LIST, N_DEV), 1)
    tall = lax.broadcasted_iota(jnp.int32, (LIST, N_DEV), 0)
    listed = jnp.broadcast_to(lists[p], (LIST, N_DEV)).astype(F32)
    slot = jnp.sum(jnp.where(wide == lax.rem(tall, 8) * 32 + tall // 8, listed, 0.0), axis=1, keepdims=True)
    slot = slot.astype(jnp.int32)
    chooser = jnp.where(wide == slot // 8, 1.0, 0.0)
    givers[p] = chooser.T.astype(BF16)
    chooser = chooser.astype(BF16)
    chosen[p] = chooser
    within = jnp.concatenate([lax.rem(fetch[p, g], 16).astype(F32) for g in range(N_CAM)], axis=1).astype(BF16)
    near = lax.dot_general(chooser, within, (((1,), (1,)), ((), ())), preferred_element_type=F32)
    eight = lax.broadcasted_iota(jnp.int32, near.shape, 1)
    column = jnp.sum(jnp.where(eight == lax.rem(slot, 8), near, 0.0), axis=1, keepdims=True)
    spot = jnp.broadcast_to(column, (LIST, 128)).astype(jnp.int32)
    spots[p] = spot
    spots_o[p] = spot + (slot // 512) * 32 + p * 16


def before_of(run):
    row = lax.broadcasted_iota(jnp.int32, (8, 128), 0)
    for s in (1, 2, 4):
        run = run * jnp.where(row >= s, pltpu.roll(run, s, 0), 1.0)
    return jnp.where(row >= 1, pltpu.roll(run, 1, 0), 1.0)


def after_of(run):
    row = lax.broadcasted_iota(jnp.int32, (8, 128), 0)
    for s in (1, 2, 4):
        run = run + jnp.where(row < 8 - s, pltpu.roll(run, 8 - s, 0), 0.0)
    return jnp.where(row < 7, pltpu.roll(run, 7, 0), 0.0)


def render(
    p, data, opacity, place_ref, count_ref, chosen, givers, spots, spots_o, target, cols, alpha_ref, through_ref, lost
):
    lane_b = lax.broadcasted_iota(jnp.int32, (BLK, 128), 1)
    row_b = lax.broadcasted_iota(jnp.int32, (BLK, 128), 0)
    lane_1 = lax.broadcasted_iota(jnp.int32, (1, 128), 1)
    blocks, parts = LIST // BLK, BLK // 8
    picked = pick(chosen[p], jnp.concatenate([data, opacity], axis=1))
    spot = spots[p]
    for k in range(8):
        cols[k] = jnp.take_along_axis(picked[:, 0:128], spot + k * 16, axis=1)
    cols[8] = jnp.take_along_axis(picked[:, 128:256], spots_o[p], axis=1)

    tile = place_ref[p]
    count = count_ref[p]
    left = (lax.rem(tile, 256) * 16).astype(F32) + 0.5
    top = ((tile // 256) * 16).astype(F32) + 0.5
    px = left + lax.rem(lane_1, 16).astype(F32)
    py = [top + ((lane_1 + h * 128) // 16).astype(F32) for h in range(2)]

    def ahead(b, carry):
        rows = pl.ds(pl.multiple_of(b * BLK, BLK), BLK)
        u, v, ca, cb, cc = [cols[k, rows, :] for k in range(5)]
        shade = [cols[k, rows, :] for k in (5, 6, 7)]
        o = cols[8, rows, :]
        live = lax.rem(row_b, 8) * 32 + row_b // 8 + b * parts < count
        dx = px - u
        dxx = ca * dx * dx
        result = []
        for h in range(2):
            run, shown = carry[h][0], list(carry[h][1:])
            dy = py[h] - v
            quad = dxx + 2.0 * cb * dx * dy + cc * dy * dy
            alpha = jnp.where(live, o * jnp.exp(-0.5 * quad), 0.0)
            alpha_ref[h, rows, :] = alpha
            keep = 1.0 - alpha
            before = []
            for n in range(parts):
                before.append(run)
                run = run * keep[8 * n : 8 * n + 8]
            before = jnp.concatenate(before, axis=0)
            through_ref[h, rows, :] = before
            weight = alpha * before
            for k in range(3):
                value = shade[k] * weight
                for n in range(parts):
                    shown[k] = shown[k] + value[8 * n : 8 * n + 8]
            result.append((run, *shown))
        return tuple(result)

    one, zero = jnp.ones((8, 128), F32), jnp.zeros((8, 128), F32)
    state = lax.fori_loop(0, blocks, ahead, ((one, zero, zero, zero),) * 2)
    ahead_of, miss, behind = [], [], []
    for h in range(2):
        prefix = before_of(state[h][0])
        parts_of = [prefix * state[h][1 + k] for k in range(3)]
        gap = [
            jnp.sum(parts_of[k], axis=0, keepdims=True) - target[p, k, :, h * 128 : (h + 1) * 128]
            for k in range(3)
        ]
        ahead_of.append(jnp.concatenate([prefix] * parts, axis=0))
        miss.append(gap)
        behind.append(after_of(gap[0] * parts_of[0] + gap[1] * parts_of[1] + gap[2] * parts_of[2]))

    def back(i, carry):
        b = blocks - 1 - i
        rows = pl.ds(pl.multiple_of(b * BLK, BLK), BLK)
        u, v, ca, cb, cc = [cols[k, rows, :] for k in range(5)]
        shade = [cols[k, rows, :] for k in (5, 6, 7)]
        o = cols[8, rows, :]
        dx = px - u
        sums = [0.0] * 9
        result = []
        for h in range(2):
            alpha = alpha_ref[h, rows, :]
            before = through_ref[h, rows, :] * ahead_of[h]
            dy = py[h] - v
            weight = alpha * before
            pull = shade[0] * miss[h][0] + shade[1] * miss[h][1] + shade[2] * miss[h][2]
            value = pull * weight
            run = carry[h]
            after = []
            for n in reversed(range(parts)):
                after.insert(0, run)
                run = run + value[8 * n : 8 * n + 8]
            result.append(run)
            after = jnp.concatenate(after, axis=0)
            slope = (before * pull - after / (1.0 - alpha)) * alpha
            tilt_x, tilt_y = slope * dx, slope * dy
            terms = [tilt_x, tilt_y, tilt_x * dx, tilt_x * dy, tilt_y * dy, slope]
            terms = terms + [weight * miss[h][k] for k in range(3)]
            sums = [x + y for x, y in zip(sums, terms)]
        m_x, m_y, m_xx, m_xy, m_yy, m_0, *g_shade = [jnp.sum(x, axis=1, keepdims=True) for x in sums]
        grads = [ca * m_x + cb * m_y, cb * m_x + cc * m_y, -0.5 * m_xx, -m_xy, -0.5 * m_yy] + g_shade
        spot_b = spots[p, rows, :]
        value = jnp.zeros((BLK, 128), F32)
        for k in range(8):
            value = jnp.where(lane_b == spot_b + k * 16, jnp.broadcast_to(grads[k], (BLK, 128)), value)
        lost[rows, 0:128] = value
        lost[rows, 128:256] = jnp.where(lane_b == spots_o[p, rows, :], m_0 / o, 0.0)
        return tuple(result)

    lax.fori_loop(0, blocks, back, tuple(behind))
    given = pick_two(givers[p], lost[...])
    by_tile = given[0:64, 128:256]
    for g in range(1, N_CAM):
        by_tile = by_tile + given[g * 64 : g * 64 + 64, 128:256]
    return given[:, 0:128], by_tile


def gradient_kernel(
    cam, pos, scl, rot, opa, col, table, back, back_o, g_pos, g_scl, g_rot, g_opa, g_col, raw, view_ref, cot, total
):
    row = lax.broadcasted_iota(jnp.int32, (8, 128), 0)
    lane = lax.broadcasted_iota(jnp.int32, (8, 128), 1)
    for k, value in enumerate(view_of(cam, row)):
        view_ref[k] = value
    start = 0
    for ref in (pos, scl, rot, opa, col):
        for j in range(8):
            raw[start : start + ref.shape[0], j, :] = ref[:, j * 128 : (j + 1) * 128]
        start += ref.shape[0]

    def fold(value, first):
        out = jnp.zeros((8, 128), F32)
        for j in range(8):
            part = jnp.take_along_axis(value[8 * j : 8 * j + 8], first + lax.rem(lane, 16), axis=1)
            part = jnp.take_along_axis(part, lane // 16, axis=0)
            out = jnp.where(row == j, part, out)
        return out

    own = lax.axis_index("cam") * 32
    shared = (back_o[0] + back_o[1]) + (back_o[2] + back_o[3])
    opacity = fold(shared, own) + fold(shared, own + 16)
    for g in range(N_CAM):
        chooser = chooser_of(table, g).T.astype(BF16)
        here = pl.ds(g * N_TILE, N_TILE)
        sent = jnp.concatenate([back[here, 0, :], back[here, 1, :]], axis=1)
        value = pick_two(chooser, sent)
        for p in range(2):
            part = value[p * 64 : p * 64 + 64, p * 128 : p * 128 + 128]
            for v in range(8):
                cot[2 * g + p, v] = fold(part, v * 16)
    for k in range(57):
        total[k] = jnp.zeros((8, 128), F32)
    shape_raw = [raw[k] for k in range(3, 10)]
    for k, value in enumerate(covariance_of(shape_raw)):
        cot[8, k] = value

    def step(v, carry):
        view = [view_ref[k, pl.ds(v, 1), :] for k in range(15)]
        point = [raw[k] for k in range(3)]
        cov = [cot[8, k] for k in range(6)]
        colors = [raw[11 + k] for k in range(48)]
        _, pull = jax.vjp(lambda a, b, d: screen_of(a, b, d, view), point, cov, colors)
        grads = pull([cot[v, k] for k in range(8)])
        for k, value in enumerate(grads[0] + grads[1] + grads[2]):
            total[k] = total[k] + value
        return carry

    lax.fori_loop(0, 8, step, 0)
    _, pull = jax.vjp(covariance_of, [raw[k] for k in range(3, 10)])
    (shape_grads,) = pull([total[3 + k] for k in range(6)])
    for k in range(7):
        total[57 + k] = shape_grads[k]
    o = sigmoid(raw[10])
    total[3] = opacity * o * (1.0 - o)
    for j in range(8):
        here = pl.ds(j * 128, 128)
        g_pos[:, here] = total[0:3, j, :]
        g_scl[:, here] = total[57:60, j, :]
        g_rot[:, here] = total[60:64, j, :]
        g_opa[:, here] = total[3:4, j, :]
        g_col[:, here] = total[9:57, j, :]


VMEM = pl.BlockSpec(memory_space=pltpu.VMEM)
SMEM = pl.BlockSpec(memory_space=pltpu.SMEM)
DMA = pltpu.SemaphoreType.DMA


def shape(*dims, dtype=F32):
    return jax.ShapeDtypeStruct(dims, dtype)


def body(
    positions,
    log_scales,
    rotations,
    opacities,
    colors,
    cameras,
    targets,
    tile_ids,
    tile_counts,
    tile_lists,
    fetch_ids,
):
    params = (positions, log_scales, rotations, opacities.reshape(1, 1024), colors)
    whole, plane = pltpu.VMEM((N_DEV, 2, 128), F32), pltpu.VMEM((N_TILE, 1, 128), F32)
    table, back, back_o = pl.pallas_call(
        main_kernel,
        out_shape=(
            shape(N_DEV, 1, 128, dtype=jnp.int32),
            shape(N_DEV, 2, 128),
            shape(N_CAM, 64, 128),
        ),
        in_specs=[SMEM] * 3 + [pl.BlockSpec(memory_space=pl.ANY)] * 8,
        out_specs=(VMEM,) * 3,
        scratch_shapes=[
            *[pltpu.VMEM((n, 1024), F32) for n in (3, 3, 4, 1, 48)],
            pltpu.VMEM((2, N_CAM, 8, N_TILE), jnp.int32),
            pltpu.VMEM((2, 1, LIST), jnp.int32),
            pltpu.VMEM((2, 3, 1, PIX), F32),
            pltpu.VMEM((1, 1, 128), jnp.int32),
            pltpu.VMEM((64, 1024), F32),
            pltpu.VMEM((512, 8, 128), F32),
            pltpu.VMEM((15, 8, 128), F32),
            pltpu.VMEM((9, 64, 128), F32),
            whole,
            plane,
            whole,
            plane,
            whole,
            plane,
            pltpu.VMEM((N_CAM, 64, 128), F32),
            plane,
            pltpu.VMEM((64, 128), F32),
            pltpu.VMEM((2, LIST, N_DEV), BF16),
            pltpu.VMEM((2, N_DEV, LIST), BF16),
            pltpu.VMEM((2, LIST, 128), jnp.int32),
            pltpu.VMEM((2, LIST, 128), jnp.int32),
            pltpu.VMEM((9, LIST, 128), F32),
            pltpu.VMEM((2, LIST, 128), F32),
            pltpu.VMEM((2, LIST, 128), F32),
            pltpu.VMEM((LIST, 2 * 128), F32),
        ]
        + [DMA] * 23
        + [DMA((8,))],
        compiler_params=pltpu.CompilerParams(collective_id=0, has_side_effects=True),
    )(
        tile_ids.reshape(2),
        tile_counts.reshape(2),
        cameras,
        *params,
        fetch_ids.reshape(2, N_CAM, N_TILE, 8).transpose(0, 1, 3, 2),
        tile_lists.reshape(2, 1, LIST),
        targets.reshape(2, 3, 1, PIX),
    )

    g_pos, g_scl, g_rot, g_opa, g_col = pl.pallas_call(
        gradient_kernel,
        out_shape=tuple(shape(n, 1024) for n in (3, 3, 4, 1, 48)),
        in_specs=[SMEM] + [VMEM] * 8,
        out_specs=(VMEM,) * 5,
        scratch_shapes=[
            pltpu.VMEM((59, 8, 128), F32),
            pltpu.VMEM((15, 8, 128), F32),
            pltpu.VMEM((9, 8, 8, 128), F32),
            pltpu.VMEM((64, 8, 128), F32),
        ],
    )(cameras, *params, table, back, back_o)
    return g_pos, g_scl, g_rot, g_opa.reshape(1024), g_col


def solution(mesh):
    return jax.shard_map(
        body,
        mesh=mesh,
        in_specs=(
            P(None, ("cam", "tile")),
            P(None, ("cam", "tile")),
            P(None, ("cam", "tile")),
            P(("cam", "tile")),
            P(None, ("cam", "tile")),
            P(),
            P(None, "cam", "tile", None, None),
            P(None, "cam", "tile"),
            P(None, "cam", "tile"),
            P(None, "cam", "tile", None),
            P(None, "cam", "tile", None, None, None),
        ),
        out_specs=(
            P(None, ("cam", "tile")),
            P(None, ("cam", "tile")),
            P(None, ("cam", "tile")),
            P(("cam", "tile")),
            P(None, ("cam", "tile")),
        ),
        check_vma=False,
    )
```
